32 devices in a mesh: pipe: 4 (over y, core), ctx: 4 (over z), dp: 2 (over x).
Axes of the slice: x: 2, y: 2, z: 4, core: 2. Of those that a mesh axis runs over, the one named last changes fastest.
Arguments:
- hidden: bfloat16 [4, 1024, 4096], P('pipe', 'ctx', 'dp'), may hold values from -64 to 64
- cotangent: bfloat16 [4, 1024, 4096], P('pipe', 'ctx', 'dp'), may hold values from -6 to 6
- gain_rows: float32 [4, 4096], P('pipe', ('dp', 'ctx')), may hold values from 0.5 to 1.5
- short_taps: float32 [4, 9, 4096], P('pipe', None, ('dp', 'ctx')), may hold values from -3.5 to 3.5
- long_taps: float32 [4, 7, 4096], P('pipe', None, ('dp', 'ctx')), may hold values from -2 to 2
Outputs:
- hidden_grad: bfloat16 [4, 1024, 4096], P('pipe', 'ctx', 'dp')
- gain_grad: float32 [4, 4096], P('pipe', ('dp', 'ctx'))
- short_grad: float32 [4, 9, 4096], P('pipe', None, ('dp', 'ctx'))
- long_grad: float32 [4, 7, 4096], P('pipe', None, ('dp', 'ctx'))
The draws below stay inside these ranges and needn't reach their ends.
All inputs are finite; a program needn't handle non-finite values.
Results may differ from the reference program's by a relative error of at most 0.0056.
Values may be sent and summed in bfloat16 or wider, within the bound.
A program may use at most 64 MiB of HBM per device.

```python
import jax
import jax.numpy as jnp
from jax import lax

WIDTH = 4096
SHORT = 3
LONG = 7
SECTIONS = 4
SEQ = 1024


def draw_hidden(key, part):
    full_shape = (SECTIONS, SEQ, WIDTH)
    key_base = jax.random.fold_in(key, 11)
    key_row = jax.random.fold_in(key, 12)
    key_col = jax.random.fold_in(key, 13)
    row_scale = jnp.exp(jax.random.uniform(key_row, (SECTIONS, SEQ, 1), jnp.float32, -1.1513, 1.1513))
    base_draw = jnp.clip(jax.random.normal(key_base, full_shape, jnp.float32), -6.0, 6.0)
    col_scale = jnp.exp(jax.random.uniform(key_col, (WIDTH,), jnp.float32, -1.1513, 1.1513))
    values = base_draw * row_scale * col_scale
    return values.astype(jnp.bfloat16)


def spiked(values, own_key, source, target, shards_of, factor):
    owner, partner = [(jnp.arange(values.shape[dim]) // (values.shape[dim] // shards_of)).reshape([-1 if axis == dim else 1 for axis in range(values.ndim)]) for dim in (source, target)]
    chosen = jax.random.permutation(own_key, shards_of)[partner]
    strong = (owner == chosen) | (owner == (partner + shards_of // 2) % shards_of)
    return jnp.where(strong, factor * values, values)


def levels(stream_key, extent, cuts, smallest, largest):
    level, own = 1.0, jax.random.fold_in(stream_key, 6)
    for axis_at, parts in cuts:
        steps = jnp.exp(jax.random.uniform(jax.random.fold_in(own, axis_at), (parts,), jnp.float32, smallest / len(cuts), largest / len(cuts)))
        level = level * jnp.repeat(steps, extent[axis_at] // parts).reshape([-1 if axis == axis_at else 1 for axis in range(len(extent))])
    return level


def centred(key, shape, width, most, cuts=(), held_as=jnp.bfloat16):
    values = width * jax.random.normal(key, shape, jnp.float32)
    if cuts:
        values = values * levels(key, shape, cuts, -0.22, 0.18)
    return jnp.clip(values, -most, most).astype(held_as)


def noise_with(own_key, extent, spread, bound, cuts, heavy, held_as=jnp.bfloat16):
    result = spread * jax.random.normal(own_key, extent, jnp.float32)
    if cuts:
        result = result * levels(own_key, extent, cuts, -0.22, 0.18)
    return jnp.clip(spiked(result, jax.random.fold_in(own_key, 3), *heavy), -bound, bound).astype(held_as)


def setup_inputs(seed: int = 0) -> dict:
    keys = jax.random.split(jax.random.key(seed), 6)
    return {
        "hidden": draw_hidden(jax.random.fold_in(keys[5], 71), 0),
        "cotangent": noise_with(keys[1], (SECTIONS, SEQ, WIDTH), 1.0, 6.0, ((0, 4), (1, 4), (2, 2)), (1, 2, 4, 2.0)),
        "gain_rows": jnp.clip(1.0 + 0.1 * jax.random.normal(keys[2], (SECTIONS, WIDTH), jnp.float32), 0.5, 1.5),
        "short_taps": centred(keys[3], (SECTIONS, 3 * SHORT, WIDTH), SHORT ** -0.5, 3.5, ((0, 4), (2, 8)), jnp.float32),
        "long_taps": centred(keys[4], (SECTIONS, LONG, WIDTH), LONG ** -0.5, 2.0, ((0, 4), (2, 8)), jnp.float32),
    }


def delayed(source, places):
    if places == 0:
        return source
    zero_rows = jnp.zeros(source.shape[:-2] + (places, source.shape[-1]), source.dtype)
    return jnp.concatenate([zero_rows, source[..., :source.shape[-2] - places, :]], axis=-2)

def hyena_block(signal, gain_row, short_filter, long_filter):
    mean_square = lax.optimization_barrier(jnp.mean(signal * signal, axis=-1, keepdims=True))
    normed = signal * lax.rsqrt(mean_square + 1e-05) * gain_row
    tap_count = short_filter.shape[0] // 3
    lagged = [delayed(normed, tap_index) for tap_index in range(tap_count)]
    streams = []
    for stream_index in range(3):
        summed = short_filter[tap_count * stream_index] * lagged[0]
        for tap_index in range(1, tap_count):
            summed = summed + short_filter[tap_count * stream_index + tap_index] * lagged[tap_index]
        streams.append(summed)
    product = streams[1] * streams[2]
    mixing = long_filter[0] * product
    for tap_index in range(1, long_filter.shape[0]):
        mixing = mixing + long_filter[tap_index] * delayed(product, tap_index)
    return signal + streams[0] * mixing

def apply_block(values, filter_set):
    return hyena_block(values, filter_set[0], filter_set[1], filter_set[2])

def section_pass(packed):
    signal, cot_next, own_set, next_set = packed
    signal_f = signal.astype(jnp.float32)
    inner = apply_block(signal_f, own_set).astype(jnp.bfloat16)
    unused, pull_outer = jax.vjp(apply_block, inner.astype(jnp.float32), next_set)
    inner_grad, next_grads = pull_outer(cot_next.astype(jnp.float32))
    unused_inner, pull_inner = jax.vjp(apply_block, signal_f, own_set)
    hidden_grad, own_grads = pull_inner(inner_grad)
    return (hidden_grad.astype(jnp.bfloat16), own_grads, next_grads)

def reference(hidden, cotangent, gain_rows, short_taps, long_taps):
    cot_next = jnp.roll(cotangent, -1, axis=0)
    own_sets = (gain_rows, short_taps, long_taps)
    next_sets = (jnp.roll(gain_rows, -1, axis=0), jnp.roll(short_taps, -1, axis=0), jnp.roll(long_taps, -1, axis=0))
    hidden_grad, own_grads, next_grads = lax.map(section_pass, (hidden, cot_next, own_sets, next_sets))
    gain_grad = own_grads[0] + jnp.roll(next_grads[0], 1, axis=0)
    short_grad = own_grads[1] + jnp.roll(next_grads[1], 1, axis=0)
    long_grad = own_grads[2] + jnp.roll(next_grads[2], 1, axis=0)
    return (hidden_grad, gain_grad, short_grad, long_grad)
```

```python
import functools

import jax
import jax.numpy as jnp
from jax import lax
from jax.experimental import pallas as pl
from jax.experimental.pallas import tpu as pltpu
from jax.sharding import PartitionSpec as P

MESH = pl.DeviceIdType.MESH
F32 = jnp.float32
BF16 = jnp.bfloat16
LANES = 128
SUB = 8
EPS = 1e-05


def kernel(
    cfg,
    hid,
    cot,
    gain_in,
    short_in,
    long_in,
    out,
    gain_out,
    short_out,
    long_out,
    hbuf,
    htop,
    hbot,
    cbuf,
    cbot,
    obuf,
    slab,
    fr,
    filt,
    fold,
    grads,
    gin,
    gs,
    rg,
    xs,
    ys,
    zs,
    wd_outer,
    wd_inner,
    saved,
    parts,
    fstate,
    bstate,
    st0_send,
    st0_recv,
    st_send,
    st_recv,
    rows,
    in_sem,
    out_sem,
    halo_send,
    halo_recv,
    c_send,
    c_recv,
    f_send,
    f_recv,
    p_send,
    p_recv,
    g_send,
    g_recv,
    s0_send,
    s0_recv,
    s_send,
    s_recv,
):
    npipe, nctx, ndp = cfg["npipe"], cfg["nctx"], cfg["ndp"]
    nrow, nb, cb, ntap, nshort, width = (
        cfg["nrow"], cfg["nb"], cfg["cb"], cfg["ntap"], cfg["nshort"], cfg["width"],
    )
    chunks = cfg["chunks"]
    taps = nshort // 3
    nlong = ntap - 1 - nshort
    halo = cfg["halo"]
    total = nrow + 2 * halo
    part = nrow // chunks
    groups = nb // SUB
    edge = halo // SUB
    octets = part // SUB
    span = octets + edge
    nfwd = taps - 1 + nlong - 1
    nbwd = nlong - 1 + 3 * (taps - 1)
    pipe, ctx, dp = lax.axis_index("pipe"), lax.axis_index("ctx"), lax.axis_index("dp")
    prev = lax.rem(pipe + npipe - 1, npipe)
    follow = lax.rem(pipe + 1, npipe)

    def ctx_at(o):
        return lax.rem(ctx + o, nctx)

    def dp_at(o):
        return lax.rem(dp + o, ndp)

    def dev(p, z, d):
        return {"pipe": p, "ctx": z, "dp": d}

    def remote(src, dst, ss, rs, where):
        return pltpu.make_async_remote_copy(
            src_ref=src, dst_ref=dst, send_sem=ss, recv_sem=rs, device_id=where, device_id_type=MESH
        )

    barrier = pltpu.get_barrier_semaphore()
    peers = [(pipe, ctx_at(o), dp) for o in range(1, nctx)]
    for d in range(1, ndp):
        for o in sorted({0, 1 % nctx, (nctx - 1) % nctx}):
            peers.append((pipe, ctx_at(o), dp_at(d)))
    peers.append((prev, ctx, dp))
    peers += [(follow, ctx_at(o), dp) for o in range(nctx)]
    for p, z, d in peers:
        pl.semaphore_signal(barrier, inc=1, device_id=dev(p, z, d), device_id_type=MESH)

    def rows_of(c):
        return pl.ds(c * part, part)

    def load_hid(c):
        return pltpu.make_async_copy(hid.at[0, rows_of(c), :], hbuf.at[rows_of(c), :], in_sem.at[c])

    for c in range(chunks):
        load_hid(c).start()

    zero = jnp.zeros((SUB, LANES), F32)
    for k in range(ntap):
        src, row = (gain_in, 0) if k == 0 else ((short_in, k - 1) if k <= nshort else (long_in, k - 1 - nshort))
        for j in range(cb):
            cols = pl.ds(j * LANES, LANES)
            piece = src[row : row + 1, cols] if k == 0 else src[row, 0:1, cols]
            slab[k * cb + j : k * cb + j + 1, :] = piece
    pad = slab.shape[0] - ntap * cb
    if pad:
        slab[ntap * cb :, :] = jnp.zeros((pad, LANES), F32)
        for z in range(nctx):
            gs[z, ntap * cb :, :] = jnp.zeros((pad, LANES), F32)
    fr[0, ctx] = slab[...]
    for i in range(2 * groups * nfwd):
        fstate[i * SUB : (i + 1) * SUB, :] = zero
    for i in range(2 * groups * nbwd):
        bstate[i * SUB : (i + 1) * SUB, :] = zero
    for i in range(2 * ntap * groups):
        grads[i // (ntap * groups), i % (ntap * groups) * SUB : (i % (ntap * groups) + 1) * SUB, :] = zero

    lane = lax.broadcasted_iota(jnp.int32, (SUB, LANES), 1)

    def spread(dst, first, block):
        for half in range(2):
            piece = block[half * SUB : (half + 1) * SUB, :]
            start = (first + half * SUB) * SUB
            for j in range(nb):
                dst[pl.ds(j // SUB * total * SUB + start + j % SUB, SUB, stride=SUB), :] = piece[:, j * LANES : (j + 1) * LANES]

    def squares(stat, first, block):
        for half in range(2):
            acc = None
            for j in range(nb):
                piece = block[half * SUB : (half + 1) * SUB, j * LANES : (j + 1) * LANES]
                acc = piece * piece if acc is None else acc + piece * piece
            value = jnp.sum(acc, axis=1, keepdims=True)
            stat = jnp.where(lane == first // SUB + half, value, stat)
        return stat

    def take_hidden(i, stat):
        block = hbuf[pl.ds(pl.multiple_of(i * 16, 16), 16), :].astype(F32)
        spread(xs, halo + i * 16, block)
        return squares(stat, halo + i * 16, block)

    stat = zero
    for c in range(chunks):
        load_hid(c).wait()
        stat = lax.fori_loop(c * part // 16, (c + 1) * part // 16, take_hidden, stat)
    st0_send[...] = stat
    st0_recv[1, dp] = stat

    pl.semaphore_wait(barrier, len(peers))

    up_z = lax.max(ctx - 1, 0)
    down_z = lax.min(ctx + 1, nctx - 1)
    head, tail = pl.ds(0, halo), pl.ds(nrow - halo, halo)
    to_bot = remote(hbuf.at[head, :], hbot, halo_send.at[0], halo_recv.at[0], dev(pipe, up_z, dp))
    to_top = remote(hbuf.at[tail, :], htop, halo_send.at[1], halo_recv.at[1], dev(pipe, down_z, dp))
    to_cbot = remote(cot.at[0, head, :], cbot, halo_send.at[2], halo_recv.at[2], dev(prev, up_z, dp))
    has_up, has_down = ctx > 0, ctx < nctx - 1

    def send_filters(b, o):
        where = dev(prev if b else pipe, ctx_at(o), dp)
        return remote(slab, fr.at[b, ctx], f_send.at[b, o], f_recv.at[b, ctx], where)

    def to_stat0(slot, o, z):
        return remote(st0_send, st0_recv.at[slot, dp], s0_send.at[slot, o], s0_recv.at[slot, dp], dev(pipe, z, dp_at(o)))

    def from_stat0(slot, o, z):
        there = dp_at(o)
        return remote(
            st0_send, st0_recv.at[slot, there], s0_send.at[slot, o], s0_recv.at[slot, there], dev(pipe, z, there)
        )

    for o in range(1, nctx):
        send_filters(0, o).start()

    @pl.when(has_down)
    def _():
        to_top.start()
        for o in range(ndp):
            to_stat0(0, o, down_z).start()

    for o in range(1, ndp):
        to_stat0(1, o, ctx).start()

    @pl.when(has_up)
    def _():
        to_bot.start()
        for o in range(ndp):
            to_stat0(2, o, up_z).start()
        to_cbot.start()

    def to_cot(c):
        return remote(
            cot.at[0, rows_of(c), :], cbuf.at[rows_of(c), :], c_send.at[c], c_recv.at[c], dev(prev, ctx, dp)
        )

    for o in range(nctx):
        send_filters(1, o).start()
    for c in range(chunks - 1, -1, -1):
        to_cot(c).start()

    @pl.when(has_up)
    def _():
        remote(htop, htop, halo_send.at[1], halo_recv.at[1], dev(pipe, up_z, dp)).wait_recv()
        for o in range(ndp):
            from_stat0(0, o, up_z).wait_recv()

    @pl.when(jnp.logical_not(has_up))
    def _():
        htop[...] = jnp.zeros(htop.shape, BF16)
        for d in range(ndp):
            st0_recv[0, d] = zero

    @pl.when(has_down)
    def _():
        remote(hbot, hbot, halo_send.at[0], halo_recv.at[0], dev(pipe, down_z, dp)).wait_recv()
        for o in range(ndp):
            from_stat0(2, o, down_z).wait_recv()

    @pl.when(jnp.logical_not(has_down))
    def _():
        hbot[...] = jnp.zeros(hbot.shape, BF16)
        for d in range(ndp):
            st0_recv[2, d] = zero

    spread(xs, 0, htop[...].astype(F32))
    spread(xs, halo + nrow, hbot[...].astype(F32))

    def row_scale(value):
        return lax.rsqrt(value / width + EPS)

    def mean_of(value):
        return value / width

    def put_rows(stage, at_octet, value, i):
        column = jnp.sum(jnp.where(lane == i, value, 0.0), axis=1, keepdims=True)
        rows[stage, pl.ds(pl.multiple_of(at_octet * SUB, SUB), SUB), :] = jnp.broadcast_to(column, (SUB, LANES))

    for o in range(1, ndp):
        from_stat0(1, o, ctx).wait_recv()
    sums = []
    for slot in range(3):
        value = st0_recv[slot, 0]
        for d in range(1, ndp):
            value = value + st0_recv[slot, d]
        sums.append(row_scale(value))
    for i in range(edge):
        put_rows(0, i, sums[0], i + nrow // SUB)
        put_rows(0, edge + nrow // SUB + i, sums[2], i + edge)
    for i in range(edge, edge + nrow // SUB):
        put_rows(0, i, sums[1], i)

    def first_octet(c):
        return jnp.where(c == 0, 0, edge + octets * c)

    def send_stat(stage, c, value):
        st_send[stage, c] = value
        st_recv[stage, c, dp] = value
        for o in range(1, ndp):
            remote(
                st_send.at[stage, c], st_recv.at[stage, c, dp], s_send.at[stage, c, o], s_recv.at[stage, c, dp],
                dev(pipe, ctx, dp_at(o)),
            ).start()

    def get_stat(stage, c, fn):
        for o in range(1, ndp):
            there = dp_at(o)
            remote(
                st_send.at[stage, c], st_recv.at[stage, c, there], s_send.at[stage, c, o], s_recv.at[stage, c, there],
                dev(pipe, ctx, there),
            ).wait()
        value = st_recv[stage, c, 0]
        for d in range(1, ndp):
            value = value + st_recv[stage, c, d]
        value = fn(value)
        base = first_octet(c)
        for k in range(span):
            put_rows(stage + 1, base + k, value, base + k)

    def collect(c):
        base = first_octet(c)
        value = zero
        for n in range(span):
            acc = None
            for g in range(groups):
                spot = g * total * SUB + (base + n) * SUB * SUB
                for k in range(SUB):
                    piece = parts[pl.ds(spot + k, SUB, stride=SUB), :]
                    acc = piece if acc is None else acc + piece
            value = jnp.where(lane == base + n, jnp.sum(acc, axis=1, keepdims=True), value)
        return value

    def build_filters(b):
        for z in range(nctx):
            for k in range(ntap):
                filt[b, k * nb + z * cb : k * nb + (z + 1) * cb, :] = fr[b, z, k * cb : (k + 1) * cb, :]
        for g in range(groups):
            gain = filt[b, g * SUB : (g + 1) * SUB, :]
            for k in range(1, 1 + nshort):
                spot = k * nb + g * SUB
                fold[b, spot - nb : spot - nb + SUB, :] = filt[b, spot : spot + SUB, :] * gain

    for o in range(1, nctx):
        there = ctx_at(o)
        remote(slab, fr.at[0, there], f_send.at[0, o], f_recv.at[0, there], dev(pipe, there, dp)).wait_recv()
    build_filters(0)

    def at(w, g):
        return pl.ds(pl.multiple_of((g * total + w) * SUB, SUB), SUB)

    def row_of(stage, w):
        return jnp.broadcast_to(rows[stage, pl.ds(w, 1), :], (SUB, LANES))

    def spot(k, g):
        return pl.ds(pl.multiple_of(k * nb + g * SUB, SUB), SUB)

    def kept(ref, b, g, count, i):
        return ref.at[pl.ds(pl.multiple_of(((b * groups + g) * count + i) * SUB, SUB), SUB), :]

    def forward(b, c, start, unroll):
        lo = jnp.where(c == 0, start, halo + part * c)
        hi = jnp.where(c == chunks - 1, total, halo + part * (c + 1))

        def group(g, _):
            short = [fold[b, spot(k, g), :] for k in range(nshort)]
            long = [filt[b, spot(1 + nshort + k, g), :] for k in range(nlong)]

            def step(it, carry):
                lag = list(carry[: taps - 1])
                past = list(carry[taps - 1 :])
                for u in range(unroll):
                    w = lo + it * unroll + u
                    x = (xs if b == 0 else ys)[at(w, g), :]
                    xh = x * row_of(b, w)
                    seq = [xh] + lag
                    streams = []
                    for j in range(3):
                        value = short[taps * j] * seq[0]
                        for i in range(1, taps):
                            value = value + short[taps * j + i] * seq[i]
                        streams.append(value)
                    products = [streams[1] * streams[2]] + past
                    mix = long[0] * products[0]
                    for i in range(1, nlong):
                        mix = mix + long[i] * products[i]
                    for n, value in enumerate((xh, streams[0], streams[1], streams[2], mix, products[0])):
                        saved[b, n, at(w, g), :] = value
                    if b == 0:
                        inner = (x + streams[0] * mix).astype(BF16).astype(F32)
                        ys[at(w, g), :] = inner
                        parts[at(w, g), :] = inner * inner
                    lag, past = seq[:-1], products[:-1]
                return tuple(lag + past)

            carry = tuple(kept(fstate, b, g, nfwd, i)[...] for i in range(nfwd))
            carry = lax.fori_loop(0, (hi - lo) // unroll, step, carry)
            for i in range(nfwd):
                kept(fstate, b, g, nfwd, i)[...] = carry[i]
            return 0

        lax.fori_loop(0, groups, group, 0)

    def ahead_inner(c, _):
        forward(0, c, 0, 8)
        send_stat(0, c, collect(c))
        return 0

    lax.fori_loop(0, chunks, ahead_inner, 0)

    for z in range(nctx):
        remote(slab, fr.at[1, z], f_send.at[1, z], f_recv.at[1, z], dev(follow, z, dp)).wait_recv()
    build_filters(1)

    def ahead_outer(c, _):
        get_stat(0, c, row_scale)
        forward(1, c, halo // 2, 8)
        return 0

    lax.fori_loop(0, chunks, ahead_outer, 0)

    @pl.when(has_down)
    def _():
        remote(cbot, cbot, halo_send.at[2], halo_recv.at[2], dev(follow, down_z, dp)).wait_recv()

    @pl.when(jnp.logical_not(has_down))
    def _():
        cbot[...] = jnp.zeros(cbot.shape, BF16)

    spread(zs, halo + nrow, cbot[...].astype(F32))

    def take_cot(i, _):
        spread(zs, halo + i * 16, cbuf[pl.ds(pl.multiple_of(i * 16, 16), 16), :].astype(F32))
        return 0

    def backward(b, c, top, unroll):
        lo = halo + part * c
        hi = lo + part

        def group(g, _):
            short = [fold[b, spot(k, g), :] for k in range(nshort)]
            long = [filt[b, spot(1 + nshort + k, g), :] for k in range(nlong)]

            def one(w, state, acc):
                dmix_next, ds_next = state
                here = at(w, g)
                up = zs[here, :]
                if b == 0:
                    up = up + row_of(1, w) * (wd_outer[here, :] - saved[1, 0, here, :] * row_of(2, w))
                    xs[here, :] = up
                xh, query, key, value, mix, product = [saved[b, n, here, :] for n in range(6)]
                dmix = [up * query] + dmix_next
                dprod = long[0] * dmix[0]
                for i in range(1, nlong):
                    dprod = dprod + long[i] * dmix[i]
                ds = [[up * mix] + ds_next[0], [dprod * value] + ds_next[1], [dprod * key] + ds_next[2]]
                weighted = None
                for j in range(3):
                    for i in range(taps):
                        term = short[taps * j + i] * ds[j][i]
                        weighted = term if weighted is None else weighted + term
                (wd_outer if b == 1 else wd_inner)[here, :] = weighted
                parts[at(w, g), :] = xh * weighted
                if acc is not None:
                    fresh = []
                    for j in range(3):
                        for i in range(taps):
                            fresh.append(acc[taps * j + i] + xh * ds[j][i])
                    for i in range(nlong):
                        fresh.append(acc[nshort + i] + product * dmix[i])
                    acc = fresh
                return (dmix[:-1], [d[:-1] for d in ds]), acc

            def flat(state):
                return tuple(state[0]) + tuple(v for d in state[1] for v in d)

            def unflat(vals):
                n = nlong - 1
                rest = vals[n:]
                m = taps - 1
                return list(vals[:n]), [list(rest[j * m : (j + 1) * m]) for j in range(3)]

            def warm(it, carry):
                state = unflat(carry)
                for u in range(unroll):
                    state, _ = one(top - 1 - it * unroll - u, state, None)
                return flat(state)

            def main(it, carry):
                state, acc = unflat(carry[:nbwd]), list(carry[nbwd:])
                for u in range(unroll):
                    state, acc = one(hi - 1 - it * unroll - u, state, acc)
                return flat(state) + tuple(acc)

            extra = jnp.where(c == chunks - 1, (top - halo - nrow) // unroll, 0)
            carry = tuple(kept(bstate, b, g, nbwd, i)[...] for i in range(nbwd))
            carry = lax.fori_loop(0, extra, warm, carry)
            carry = carry + tuple(grads[b, spot(k, g), :] for k in range(1, ntap))
            carry = lax.fori_loop(0, part // unroll, main, carry)
            for i in range(nbwd):
                kept(bstate, b, g, nbwd, i)[...] = carry[i]
            for k in range(1, ntap):
                grads[b, spot(k, g), :] = carry[nbwd + k - 1]
            return 0

        lax.fori_loop(0, groups, group, 0)

    def back_outer(it, _):
        c = chunks - 1 - it
        remote(
            cbuf.at[rows_of(c), :], cbuf.at[rows_of(c), :], c_send.at[c], c_recv.at[c], dev(follow, ctx, dp)
        ).wait_recv()
        lax.fori_loop(c * (part // 16), (c + 1) * (part // 16), take_cot, 0)
        backward(1, c, total, 8)
        send_stat(1, c, collect(c))
        return 0

    lax.fori_loop(0, chunks, back_outer, 0)

    def finish_grads(b):
        for g in range(groups):
            gain = filt[b, spot(0, g), :]
            acc = None
            for k in range(1, 1 + nshort):
                raw = grads[b, spot(k, g), :]
                term = raw * filt[b, spot(k, g), :]
                acc = term if acc is None else acc + term
                grads[b, spot(k, g), :] = raw * gain
            grads[b, spot(0, g), :] = acc

    finish_grads(1)
    to_follow = remote(grads.at[1], gin, p_send.at[0], p_recv.at[0], dev(follow, ctx, dp))
    to_follow.start()

    def back_inner(it, _):
        c = chunks - 1 - it
        get_stat(1, c, mean_of)
        backward(0, c, halo + nrow + halo // 2, 8)
        send_stat(2, c, collect(c))
        return 0

    lax.fori_loop(0, chunks, back_inner, 0)

    finish_grads(0)
    remote(grads.at[1], gin, p_send.at[0], p_recv.at[0], dev(prev, ctx, dp)).wait_recv()
    for z in range(nctx):
        for k in range(ntap):
            here = pl.ds(k * nb + z * cb, cb)
            gs[z, k * cb : (k + 1) * cb, :] = grads[0, here, :] + gin[here, :]

    def send_grads(o):
        z = ctx_at(o)
        return remote(gs.at[z], rg.at[ctx], g_send.at[o], g_recv.at[ctx], dev(pipe, z, dp))

    for o in range(1, nctx):
        send_grads(o).start()
    rg[ctx] = gs[ctx]

    def finish(i, _):
        w = halo + i * 16
        halves = [pl.multiple_of(w + half * SUB, SUB) for half in range(2)]
        scales = [rows[0, pl.ds(h, SUB), :] for h in halves]
        means = [rows[3, pl.ds(h, SUB), :] for h in halves]
        for j in range(nb):
            pieces = []
            for half in range(2):
                here = pl.ds(j // SUB * total * SUB + halves[half] * SUB + j % SUB, SUB, stride=SUB)
                pieces.append(xs[here, :] + scales[half] * (wd_inner[here, :] - saved[0, 0, here, :] * means[half]))
            obuf[pl.ds(pl.multiple_of(i * 16, 16), 16), j * LANES : (j + 1) * LANES] = jnp.concatenate(
                pieces, axis=0
            ).astype(BF16)
        return 0

    def store_out(c):
        return pltpu.make_async_copy(obuf.at[rows_of(c), :], out.at[0, rows_of(c), :], out_sem.at[c])

    def wind_up(it, _):
        c = chunks - 1 - it
        get_stat(2, c, mean_of)
        lax.fori_loop(c * (part // 16), (c + 1) * (part // 16), finish, 0)
        store_out(c).start()
        return 0

    lax.fori_loop(0, chunks, wind_up, 0)

    for o in range(1, nctx):
        z = ctx_at(o)
        remote(gs.at[z], rg.at[z], g_send.at[o], g_recv.at[z], dev(pipe, z, dp)).wait_recv()
    result = rg[0]
    for z in range(1, nctx):
        result = result + rg[z]
    for k in range(ntap):
        for j in range(cb):
            cols = pl.ds(j * LANES, LANES)
            piece = result[k * cb + j : k * cb + j + 1, :]
            if k == 0:
                gain_out[0:1, cols] = piece
            elif k <= nshort:
                short_out[k - 1, 0:1, cols] = piece
            else:
                long_out[k - 1 - nshort, 0:1, cols] = piece

    for c in range(chunks):
        store_out(c).wait()
        to_cot(c).wait_send()

    @pl.when(has_up)
    def _():
        to_bot.wait_send()
        to_cbot.wait_send()
        for o in range(ndp):
            to_stat0(2, o, up_z).wait_send()

    @pl.when(has_down)
    def _():
        to_top.wait_send()
        for o in range(ndp):
            to_stat0(0, o, down_z).wait_send()

    for o in range(1, ndp):
        to_stat0(1, o, ctx).wait_send()
    for o in range(1, nctx):
        send_filters(0, o).wait_send()
        send_grads(o).wait_send()
    for o in range(nctx):
        send_filters(1, o).wait_send()
    to_follow.wait_send()


def handed_on(a0, a1, a2, a3, b0, b1, b2, b3):
    b0[...] = a0[...]

    @pl.when(pl.program_id(0) == 0)
    def _():
        b1[...] = a1[...]
        b2[...] = a2[...]
        b3[...] = a3[...]


def swap(values):
    return jnp.transpose(values, (1, 0, 2))


def per_device(mesh, hidden, cotangent, gain_rows, short_taps, long_taps):
    npipe, nctx, ndp = mesh.shape["pipe"], mesh.shape["ctx"], mesh.shape["dp"]
    nrow, chans = hidden.shape[1], hidden.shape[2]
    own = gain_rows.shape[1]
    wide = -(-own // LANES) * LANES
    nshort, nlong = short_taps.shape[1], long_taps.shape[1]
    ntap = 1 + nshort + nlong
    cb = wide // LANES
    nb = nctx * cb
    halo = 2 * (nshort // 3 + nlong - 2)
    total = nrow + 2 * halo
    slab_rows = -(-ntap * cb // SUB) * SUB
    chunks = next(n for n in (4, 2, 1) if nrow % (16 * n) == 0)
    groups = nb // SUB
    nfwd = nshort // 3 - 1 + nlong - 1
    nbwd = nlong - 1 + 3 * (nshort // 3 - 1)

    def widen(values):
        if wide == own:
            return values
        lead = values.shape[:-1]
        blocks = values.reshape(lead + (-1, own))
        blocks = jnp.pad(blocks, [(0, 0)] * (len(lead) + 1) + [(0, wide - own)])
        return blocks.reshape(lead + (-1,))

    def narrow(values):
        if wide == own:
            return values
        lead = values.shape[:-1]
        return values.reshape(lead + (-1, wide))[..., :own].reshape(lead + (-1,))

    cfg = dict(
        npipe=npipe, nctx=nctx, ndp=ndp, nrow=nrow, nb=nb, cb=cb, ntap=ntap, nshort=nshort,
        width=float(chans * ndp), halo=halo, chunks=chunks,
    )
    full = nb * LANES
    dma = pltpu.SemaphoreType.DMA
    vmem = pl.BlockSpec(memory_space=pltpu.VMEM)
    anywhere = pl.BlockSpec(memory_space=pl.ANY)
    shapes = (
        jax.ShapeDtypeStruct((1, nrow, full), BF16),
        jax.ShapeDtypeStruct((1, wide), F32),
        jax.ShapeDtypeStruct((nshort, 1, wide), F32),
        jax.ShapeDtypeStruct((nlong, 1, wide), F32),
    )
    outs = pl.pallas_call(
        functools.partial(kernel, cfg),
        out_shape=shapes,
        in_specs=[anywhere, anywhere, vmem, vmem, vmem],
        out_specs=(anywhere, vmem, vmem, vmem),
        scratch_shapes=[
            pltpu.VMEM((nrow, full), BF16),
            pltpu.VMEM((halo, full), BF16),
            pltpu.VMEM((halo, full), BF16),
            pltpu.VMEM((nrow, full), BF16),
            pltpu.VMEM((halo, full), BF16),
            pltpu.VMEM((nrow, full), BF16),
            pltpu.VMEM((slab_rows, LANES), F32),
            pltpu.VMEM((2, nctx, slab_rows, LANES), F32),
            pltpu.VMEM((2, ntap * nb, LANES), F32),
            pltpu.VMEM((2, nshort * nb, LANES), F32),
            pltpu.VMEM((2, ntap * nb, LANES), F32),
            pltpu.VMEM((ntap * nb, LANES), F32),
            pltpu.VMEM((nctx, slab_rows, LANES), F32),
            pltpu.VMEM((nctx, slab_rows, LANES), F32),
            pltpu.VMEM((total * nb, LANES), F32),
            pltpu.VMEM((total * nb, LANES), F32),
            pltpu.VMEM((total * nb, LANES), F32),
            pltpu.VMEM((total * nb, LANES), F32),
            pltpu.VMEM((total * nb, LANES), F32),
            pltpu.VMEM((2, 6, total * nb, LANES), F32),
            pltpu.VMEM((total * nb, LANES), F32),
            pltpu.VMEM((2 * groups * nfwd * SUB, LANES), F32),
            pltpu.VMEM((2 * groups * nbwd * SUB, LANES), F32),
            pltpu.VMEM((SUB, LANES), F32),
            pltpu.VMEM((3, ndp, SUB, LANES), F32),
            pltpu.VMEM((3, chunks, SUB, LANES), F32),
            pltpu.VMEM((3, chunks, ndp, SUB, LANES), F32),
            pltpu.VMEM((4, total, LANES), F32),
            dma((chunks,)),
            dma((chunks,)),
            dma((3,)),
            dma((3,)),
            dma((chunks,)),
            dma((chunks,)),
            dma((2, nctx)),
            dma((2, nctx)),
            dma((1,)),
            dma((1,)),
            dma((nctx,)),
            dma((nctx,)),
            dma((3, ndp)),
            dma((3, ndp)),
            dma((3, chunks, ndp)),
            dma((3, chunks, ndp)),
        ],
        compiler_params=pltpu.CompilerParams(
            collective_id=0, has_side_effects=True, vmem_limit_bytes=56 * 1024 * 1024
        ),
        name="relay",
    )(widen(hidden), widen(cotangent), widen(gain_rows), swap(widen(short_taps)), swap(widen(long_taps)))
    passed = [pl.BlockSpec((1, nrow // 2, full), lambda i: (0, i, 0))] + [
        pl.BlockSpec(o.shape, functools.partial(lambda rank, i: (0,) * rank, len(o.shape))) for o in shapes[1:]
    ]
    outs = pl.pallas_call(
        handed_on,
        out_shape=shapes,
        grid=(2,),
        in_specs=passed,
        out_specs=tuple(passed),
        name="handed_on",
    )(*outs)
    return tuple(narrow(o) for o in (outs[0], outs[1], swap(outs[2]), swap(outs[3])))


def solution(mesh):
    in_specs = (
        P("pipe", "ctx", "dp"),
        P("pipe", "ctx", "dp"),
        P("pipe", ("dp", "ctx")),
        P("pipe", None, ("dp", "ctx")),
        P("pipe", None, ("dp", "ctx")),
    )
    out_specs = (
        P("pipe", "ctx", "dp"),
        P("pipe", ("dp", "ctx")),
        P("pipe", None, ("dp", "ctx")),
        P("pipe", None, ("dp", "ctx")),
    )
    return jax.shard_map(
        functools.partial(per_device, mesh), mesh=mesh, in_specs=in_specs, out_specs=out_specs, check_vma=False
    )
```

```python
import functools

import jax
import jax.numpy as jnp
from jax import lax
from jax.experimental import pallas as pl
from jax.experimental.pallas import tpu as pltpu
from jax.sharding import PartitionSpec as P

MESH = pl.DeviceIdType.MESH
F32 = jnp.float32
BF16 = jnp.bfloat16
LANES = 128
SUB = 8
EPS = 1e-05
BACK = 2


def kernel(
    cfg,
    hid,
    cot,
    gain_in,
    short_in,
    long_in,
    out,
    gain_out,
    short_out,
    long_out,
    hbuf,
    htop,
    hbot,
    cbuf,
    cbot,
    slab,
    fr,
    filt,
    fold,
    grads,
    gin,
    gs,
    gsent,
    rg,
    xs,
    ys,
    zs,
    wd_outer,
    wd_inner,
    saved,
    parts,
    fstate,
    bstate,
    st0_send,
    st0_recv,
    st_send,
    st_recv,
    rows,
    in_sem,
    halo_send,
    halo_recv,
    c_send,
    c_recv,
    f_send,
    f_recv,
    p_send,
    p_recv,
    g_send,
    g_recv,
    s0_send,
    s0_recv,
    s_send,
    s_recv,
):
    npipe, nctx, ndp = cfg["npipe"], cfg["nctx"], cfg["ndp"]
    nrow, nb, cb, ntap, nshort, width = (
        cfg["nrow"], cfg["nb"], cfg["cb"], cfg["ntap"], cfg["nshort"], cfg["width"],
    )
    ahead, chunks = cfg["ahead"], cfg["chunks"]
    taps = nshort // 3
    nlong = ntap - 1 - nshort
    halo = cfg["halo"]
    total = nrow + 2 * halo
    part = nrow // chunks
    groups = nb // SUB
    edge = halo // SUB
    slabs = SUB // cb if cb < SUB and SUB % cb == 0 else nctx
    slabs = min(slabs, nctx)
    teams = nctx // slabs
    nfwd = taps - 1 + nlong - 1
    nbwd = nlong - 1 + 3 * (taps - 1)
    pipe, ctx, dp = lax.axis_index("pipe"), lax.axis_index("ctx"), lax.axis_index("dp")
    prev = lax.rem(pipe + npipe - 1, npipe)
    follow = lax.rem(pipe + 1, npipe)

    def ctx_at(o):
        return lax.rem(ctx + o, nctx)

    def dp_at(o):
        return lax.rem(dp + o, ndp)

    def team_at(o):
        team = lax.rem(ctx // slabs + o // slabs, teams)
        return team * slabs + lax.rem(lax.rem(ctx, slabs) + o % slabs, slabs)

    def dev(p, z, d):
        return {"pipe": p, "ctx": z, "dp": d}

    def remote(src, dst, ss, rs, where):
        return pltpu.make_async_remote_copy(
            src_ref=src, dst_ref=dst, send_sem=ss, recv_sem=rs, device_id=where, device_id_type=MESH
        )

    barrier = pltpu.get_barrier_semaphore()
    peers = [(pipe, ctx_at(o), dp) for o in range(1, nctx)]
    for d in range(1, ndp):
        for o in sorted({0, 1 % nctx, (nctx - 1) % nctx}):
            peers.append((pipe, ctx_at(o), dp_at(d)))
    peers += [(prev, ctx, dp), (follow, ctx, dp), (follow, ctx_at(1), dp)]
    for p, z, d in peers:
        pl.semaphore_signal(barrier, inc=1, device_id=dev(p, z, d), device_id_type=MESH)

    def rows_of(c):
        return pl.ds(c * part, part)

    def load_hid(c):
        return pltpu.make_async_copy(hid.at[0, rows_of(c), :], hbuf.at[rows_of(c), :], in_sem.at[c])

    for c in range(chunks):
        load_hid(c).start()

    zero = jnp.zeros((SUB, LANES), F32)
    for k in range(ntap):
        src, row = (gain_in, 0) if k == 0 else ((short_in, k - 1) if k <= nshort else (long_in, k - 1 - nshort))
        for j in range(cb):
            cols = pl.ds(j * LANES, LANES)
            piece = src[row : row + 1, cols] if k == 0 else src[row, 0:1, cols]
            slab[k * cb + j : k * cb + j + 1, :] = piece
    pad = slab.shape[0] - ntap * cb
    if pad:
        slab[ntap * cb :, :] = jnp.zeros((pad, LANES), F32)
        for z in range(nctx):
            gs[z, ntap * cb :, :] = jnp.zeros((pad, LANES), F32)
    fr[0, ctx] = slab[...]
    for i in range(2 * groups * nfwd):
        fstate[i * SUB : (i + 1) * SUB, :] = zero
    for i in range(2 * groups * nbwd):
        bstate[i * SUB : (i + 1) * SUB, :] = zero
    for i in range(2 * ntap * groups):
        grads[i // (ntap * groups), i % (ntap * groups) * SUB : (i % (ntap * groups) + 1) * SUB, :] = zero

    lane = lax.broadcasted_iota(jnp.int32, (SUB, LANES), 1)

    def spread(dst, first, block):
        for half in range(2):
            piece = block[half * SUB : (half + 1) * SUB, :]
            start = (first + half * SUB) * SUB
            for j in range(nb):
                dst[pl.ds(j // SUB * total * SUB + start + j % SUB, SUB, stride=SUB), :] = piece[:, j * LANES : (j + 1) * LANES]

    def squares(stat, first, block):
        for half in range(2):
            acc = None
            for j in range(nb):
                piece = block[half * SUB : (half + 1) * SUB, j * LANES : (j + 1) * LANES]
                acc = piece * piece if acc is None else acc + piece * piece
            value = jnp.sum(acc, axis=1, keepdims=True)
            stat = jnp.where(lane == first // SUB + half, value, stat)
        return stat

    def take_hidden(i, stat):
        block = hbuf[pl.ds(pl.multiple_of(i * 16, 16), 16), :].astype(F32)
        spread(xs, halo + i * 16, block)
        return squares(stat, halo + i * 16, block)

    stat = zero
    for c in range(chunks):
        load_hid(c).wait()
        stat = lax.fori_loop(c * part // 16, (c + 1) * part // 16, take_hidden, stat)
    st0_send[...] = stat
    st0_recv[1, dp] = stat

    pl.semaphore_wait(barrier, len(peers))

    up_z = lax.max(ctx - 1, 0)
    down_z = lax.min(ctx + 1, nctx - 1)
    head, tail = pl.ds(0, halo), pl.ds(nrow - halo, halo)
    to_bot = remote(hbuf.at[head, :], hbot, halo_send.at[0], halo_recv.at[0], dev(pipe, up_z, dp))
    to_top = remote(hbuf.at[tail, :], htop, halo_send.at[1], halo_recv.at[1], dev(pipe, down_z, dp))
    to_cbot = remote(cot.at[0, head, :], cbot, halo_send.at[2], halo_recv.at[2], dev(prev, up_z, dp))
    has_up, has_down = ctx > 0, ctx < nctx - 1

    def send_filters(b, o):
        mine = fr.at[1, ctx] if b else slab
        return remote(mine, fr.at[b, ctx], f_send.at[b, o], f_recv.at[b, ctx], dev(pipe, team_at(o), dp))

    def wait_filters(b, o):
        there = team_at(o)
        remote(slab, fr.at[b, there], f_send.at[b, o], f_recv.at[b, there], dev(pipe, there, dp)).wait_recv()

    to_prev = remote(slab, fr.at[1, ctx], f_send.at[1, 0], f_recv.at[1, ctx], dev(prev, ctx, dp))

    def to_stat0(slot, o, z):
        return remote(st0_send, st0_recv.at[slot, dp], s0_send.at[slot, o], s0_recv.at[slot, dp], dev(pipe, z, dp_at(o)))

    def from_stat0(slot, o, z):
        there = dp_at(o)
        return remote(
            st0_send, st0_recv.at[slot, there], s0_send.at[slot, o], s0_recv.at[slot, there], dev(pipe, z, there)
        )

    for o in range(1, nctx):
        send_filters(0, o).start()

    @pl.when(has_down)
    def _():
        to_top.start()
        for o in range(ndp):
            to_stat0(0, o, down_z).start()

    for o in range(1, ndp):
        to_stat0(1, o, ctx).start()

    @pl.when(has_up)
    def _():
        to_bot.start()
        for o in range(ndp):
            to_stat0(2, o, up_z).start()
        to_cbot.start()

    def to_cot(c):
        return remote(
            cot.at[0, rows_of(c), :], cbuf.at[rows_of(c), :], c_send.at[c], c_recv.at[c], dev(prev, ctx, dp)
        )

    to_prev.start()
    for c in range(chunks - 1, -1, -1):
        to_cot(c).start()

    @pl.when(has_up)
    def _():
        remote(htop, htop, halo_send.at[1], halo_recv.at[1], dev(pipe, up_z, dp)).wait_recv()
        for o in range(ndp):
            from_stat0(0, o, up_z).wait_recv()

    @pl.when(jnp.logical_not(has_up))
    def _():
        htop[...] = jnp.zeros(htop.shape, BF16)
        for d in range(ndp):
            st0_recv[0, d] = zero

    @pl.when(has_down)
    def _():
        remote(hbot, hbot, halo_send.at[0], halo_recv.at[0], dev(pipe, down_z, dp)).wait_recv()
        for o in range(ndp):
            from_stat0(2, o, down_z).wait_recv()

    @pl.when(jnp.logical_not(has_down))
    def _():
        hbot[...] = jnp.zeros(hbot.shape, BF16)
        for d in range(ndp):
            st0_recv[2, d] = zero

    remote(slab, fr.at[1, ctx], f_send.at[1, 0], f_recv.at[1, ctx], dev(follow, ctx, dp)).wait_recv()
    for o in range(1, nctx):
        send_filters(1, o).start()

    spread(xs, 0, htop[...].astype(F32))
    spread(xs, halo + nrow, hbot[...].astype(F32))

    def row_scale(value):
        return lax.rsqrt(value / width + EPS)

    def mean_of(value):
        return value / width

    def put_rows(stage, at_octet, value, i):
        column = jnp.sum(jnp.where(lane == i, value, 0.0), axis=1, keepdims=True)
        rows[stage, pl.ds(pl.multiple_of(at_octet * SUB, SUB), SUB), :] = jnp.broadcast_to(column, (SUB, LANES))

    for o in range(1, ndp):
        from_stat0(1, o, ctx).wait_recv()
    sums = []
    for slot in range(3):
        value = st0_recv[slot, 0]
        for d in range(1, ndp):
            value = value + st0_recv[slot, d]
        sums.append(row_scale(value))
    for i in range(edge):
        put_rows(0, i, sums[0], i + nrow // SUB)
        put_rows(0, edge + nrow // SUB + i, sums[2], i + edge)
    for i in range(edge, edge + nrow // SUB):
        put_rows(0, i, sums[1], i)

    def first_octet(many, c):
        return jnp.where(c == 0, 0, edge + nrow // SUB // many * c)

    def span(many):
        return nrow // SUB // many + edge

    def send_stat(stage, c, value):
        st_send[stage, c] = value
        st_recv[stage, c, dp] = value
        for o in range(1, ndp):
            remote(
                st_send.at[stage, c], st_recv.at[stage, c, dp], s_send.at[stage, c, o], s_recv.at[stage, c, dp],
                dev(pipe, ctx, dp_at(o)),
            ).start()

    def get_stat(stage, many, c, fn):
        for o in range(1, ndp):
            there = dp_at(o)
            remote(
                st_send.at[stage, c], st_recv.at[stage, c, there], s_send.at[stage, c, o], s_recv.at[stage, c, there],
                dev(pipe, ctx, there),
            ).wait()
        value = st_recv[stage, c, 0]
        for d in range(1, ndp):
            value = value + st_recv[stage, c, d]
        value = fn(value)
        base = first_octet(many, c)
        for k in range(span(many)):
            put_rows(stage + 1, base + k, value, base + k)

    def collect(many, c):
        base = first_octet(many, c)
        value = zero
        for n in range(span(many)):
            acc = None
            for g in range(groups):
                spot = g * total * SUB + (base + n) * SUB * SUB
                for k in range(SUB):
                    piece = parts[pl.ds(spot + k, SUB, stride=SUB), :]
                    acc = piece if acc is None else acc + piece
            value = jnp.where(lane == base + n, jnp.sum(acc, axis=1, keepdims=True), value)
        return value

    per = groups // teams

    def spot(k, g):
        return pl.ds(pl.multiple_of(k * nb + g * SUB, SUB), SUB)

    def build_filters(b, team):
        for n in range(per):
            g = team * per + n
            first = n * SUB // cb
            many = max(SUB // cb, 1)
            for k in range(ntap):
                if cb >= SUB:
                    z, row = n * SUB // cb, n * SUB % cb
                    value = fr[b, team * slabs + z, k * cb + row : k * cb + row + SUB, :]
                else:
                    value = jnp.concatenate(
                        [fr[b, team * slabs + first + s, k * cb : (k + 1) * cb, :] for s in range(many)], axis=0
                    )
                filt[b, spot(k, g), :] = value
                if k == 0:
                    gain = value
                elif k <= nshort:
                    fold[b, spot(k - 1, g), :] = value * gain

    def at(w, g):
        return pl.ds(pl.multiple_of((g * total + w) * SUB, SUB), SUB)

    def row_of(stage, w):
        return jnp.broadcast_to(rows[stage, pl.ds(w, 1), :], (SUB, LANES))

    def kept(ref, b, g, count, i):
        return ref.at[pl.ds(pl.multiple_of(((b * groups + g) * count + i) * SUB, SUB), SUB), :]

    def forward(b, c, start, unroll):
        part, chunks = nrow // ahead, ahead
        lo = jnp.where(c == 0, start, halo + part * c)
        hi = jnp.where(c == chunks - 1, total, halo + part * (c + 1))

        def group(g, _):
            short = [fold[b, spot(k, g), :] for k in range(nshort)]
            long = [filt[b, spot(1 + nshort + k, g), :] for k in range(nlong)]

            def step(it, carry):
                lag = list(carry[: taps - 1])
                past = list(carry[taps - 1 :])
                for u in range(unroll):
                    w = lo + it * unroll + u
                    x = (xs if b == 0 else ys)[at(w, g), :]
                    xh = x * row_of(b, w)
                    seq = [xh] + lag
                    streams = []
                    for j in range(3):
                        value = short[taps * j] * seq[0]
                        for i in range(1, taps):
                            value = value + short[taps * j + i] * seq[i]
                        streams.append(value)
                    products = [streams[1] * streams[2]] + past
                    mix = long[0] * products[0]
                    for i in range(1, nlong):
                        mix = mix + long[i] * products[i]
                    for n, value in enumerate((xh, streams[0], streams[1], streams[2], mix, products[0])):
                        saved[b, n, at(w, g), :] = value
                    if b == 0:
                        inner = (x + streams[0] * mix).astype(BF16).astype(F32)
                        ys[at(w, g), :] = inner
                        parts[at(w, g), :] = inner * inner
                    lag, past = seq[:-1], products[:-1]
                return tuple(lag + past)

            carry = tuple(kept(fstate, b, g, nfwd, i)[...] for i in range(nfwd))
            carry = lax.fori_loop(0, (hi - lo) // unroll, step, carry)
            for i in range(nfwd):
                kept(fstate, b, g, nfwd, i)[...] = carry[i]
            return 0

        lax.fori_loop(0, groups, group, 0)

    for o in range(1, nctx):
        wait_filters(0, o)
    for n in range(teams):
        build_filters(0, n)

    def ahead_inner(c, _):
        forward(0, c, 0, 16)
        send_stat(0, c, collect(ahead, c))
        return 0

    lax.fori_loop(0, ahead, ahead_inner, 0)

    for o in range(1, nctx):
        wait_filters(1, o)
    for n in range(teams):
        build_filters(1, n)

    def ahead_outer(c, _):
        get_stat(0, ahead, c, row_scale)
        forward(1, c, 0, 16)
        return 0

    lax.fori_loop(0, ahead, ahead_outer, 0)

    @pl.when(has_down)
    def _():
        remote(cbot, cbot, halo_send.at[2], halo_recv.at[2], dev(follow, down_z, dp)).wait_recv()

    @pl.when(jnp.logical_not(has_down))
    def _():
        cbot[...] = jnp.zeros(cbot.shape, BF16)

    spread(zs, halo + nrow, cbot[...].astype(F32))

    def take_cot(i, _):
        spread(zs, halo + i * 16, cbuf[pl.ds(pl.multiple_of(i * 16, 16), 16), :].astype(F32))
        return 0

    def backward(b, c, top, brief, unroll):
        lo = halo + part * c
        hi = lo + part

        def group(g, _):
            short = [fold[b, spot(k, g), :] for k in range(nshort)]
            long = [filt[b, spot(1 + nshort + k, g), :] for k in range(nlong)]

            def one(w, state, acc):
                dmix_next, ds_next = state
                here = at(w, g)
                up = zs[here, :]
                if b == 0:
                    up = up + row_of(1, w) * (wd_outer[here, :] - saved[1, 0, here, :] * row_of(2, w))
                    xs[here, :] = up
                xh, query, key, value, mix, product = [saved[b, n, here, :] for n in range(6)]
                dmix = [up * query] + dmix_next
                dprod = long[0] * dmix[0]
                for i in range(1, nlong):
                    dprod = dprod + long[i] * dmix[i]
                ds = [[up * mix] + ds_next[0], [dprod * value] + ds_next[1], [dprod * key] + ds_next[2]]
                weighted = None
                for j in range(3):
                    for i in range(taps):
                        term = short[taps * j + i] * ds[j][i]
                        weighted = term if weighted is None else weighted + term
                (wd_outer if b == 1 else wd_inner)[here, :] = weighted
                parts[at(w, g), :] = xh * weighted
                if acc is not None:
                    fresh = []
                    for j in range(3):
                        for i in range(taps):
                            fresh.append(acc[taps * j + i] + xh * ds[j][i])
                    for i in range(nlong):
                        fresh.append(acc[nshort + i] + product * dmix[i])
                    acc = fresh
                return (dmix[:-1], [d[:-1] for d in ds]), acc

            def flat(state):
                return tuple(state[0]) + tuple(v for d in state[1] for v in d)

            def unflat(vals):
                n = nlong - 1
                rest = vals[n:]
                m = taps - 1
                return list(vals[:n]), [list(rest[j * m : (j + 1) * m]) for j in range(3)]

            def warm(it, carry):
                state = unflat(carry)
                for u in range(brief):
                    state, _ = one(top - 1 - it * brief - u, state, None)
                return flat(state)

            def main(it, carry):
                state, acc = unflat(carry[:nbwd]), list(carry[nbwd:])
                for u in range(unroll):
                    state, acc = one(hi - 1 - it * unroll - u, state, acc)
                return flat(state) + tuple(acc)

            extra = jnp.where(c == chunks - 1, (top - halo - nrow) // brief, 0)
            carry = tuple(kept(bstate, b, g, nbwd, i)[...] for i in range(nbwd))
            carry = lax.fori_loop(0, extra, warm, carry)
            carry = carry + tuple(grads[b, spot(k, g), :] for k in range(1, ntap))
            carry = lax.fori_loop(0, part // unroll, main, carry)
            for i in range(nbwd):
                kept(bstate, b, g, nbwd, i)[...] = carry[i]
            for k in range(1, ntap):
                grads[b, spot(k, g), :] = carry[nbwd + k - 1]
            return 0

        lax.fori_loop(0, groups, group, 0)

    def back_outer(it, _):
        c = chunks - 1 - it
        remote(
            cbuf.at[rows_of(c), :], cbuf.at[rows_of(c), :], c_send.at[c], c_recv.at[c], dev(follow, ctx, dp)
        ).wait_recv()
        lax.fori_loop(c * (part // 16), (c + 1) * (part // 16), take_cot, 0)
        backward(1, c, total, 8, 16)
        send_stat(1, c, collect(chunks, c))
        return 0

    lax.fori_loop(0, chunks, back_outer, 0)

    def finish_grads(b):
        for g in range(groups):
            gain = filt[b, spot(0, g), :]
            acc = None
            for k in range(1, 1 + nshort):
                raw = grads[b, spot(k, g), :]
                term = raw * filt[b, spot(k, g), :]
                acc = term if acc is None else acc + term
                grads[b, spot(k, g), :] = raw * gain
            grads[b, spot(0, g), :] = acc

    finish_grads(1)
    to_follow = remote(grads.at[1], gin, p_send.at[0], p_recv.at[0], dev(follow, ctx, dp))
    to_follow.start()

    def send_grads(o):
        z = ctx_at(o)
        return remote(gsent.at[z], rg.at[ctx], g_send.at[o], g_recv.at[ctx], dev(pipe, z, dp))

    def share_grads():
        finish_grads(0)
        remote(grads.at[1], gin, p_send.at[0], p_recv.at[0], dev(prev, ctx, dp)).wait_recv()
        for z in range(nctx):
            for k in range(ntap):
                here = pl.ds(k * nb + z * cb, cb)
                gs[z, k * cb : (k + 1) * cb, :] = grads[0, here, :] + gin[here, :]
            gsent[z] = gs[z].astype(BF16)
        for o in range(1, nctx):
            send_grads(o).start()

    def back_inner(it, _):
        c = chunks - 1 - it
        get_stat(1, chunks, c, mean_of)
        backward(0, c, halo + nrow + halo // 2, 8, 16)

        @pl.when(c == 0)
        def _():
            share_grads()

        send_stat(2, c, collect(chunks, c))
        return 0

    lax.fori_loop(0, chunks, back_inner, 0)

    def finish(i, _):
        w = halo + i * 16
        halves = [pl.multiple_of(w + half * SUB, SUB) for half in range(2)]
        scales = [rows[0, pl.ds(h, SUB), :] for h in halves]
        means = [rows[3, pl.ds(h, SUB), :] for h in halves]
        for j in range(nb):
            pieces = []
            for half in range(2):
                here = pl.ds(j // SUB * total * SUB + halves[half] * SUB + j % SUB, SUB, stride=SUB)
                pieces.append(xs[here, :] + scales[half] * (wd_inner[here, :] - saved[0, 0, here, :] * means[half]))
            out[0, pl.ds(pl.multiple_of(i * 16, 16), 16), j * LANES : (j + 1) * LANES] = jnp.concatenate(
                pieces, axis=0
            ).astype(BF16)
        return 0

    def wind_up(it, _):
        c = chunks - 1 - it
        get_stat(2, chunks, c, mean_of)
        lax.fori_loop(c * (part // 16), (c + 1) * (part // 16), finish, 0)
        return 0

    lax.fori_loop(0, chunks, wind_up, 0)

    for o in range(1, nctx):
        z = ctx_at(o)
        remote(gsent.at[z], rg.at[z], g_send.at[o], g_recv.at[z], dev(pipe, z, dp)).wait_recv()
    result = gs[ctx]
    for o in range(1, nctx):
        result = result + rg[ctx_at(o)].astype(F32)
    for k in range(ntap):
        for j in range(cb):
            cols = pl.ds(j * LANES, LANES)
            piece = result[k * cb + j : k * cb + j + 1, :]
            if k == 0:
                gain_out[0:1, cols] = piece
            elif k <= nshort:
                short_out[k - 1, 0:1, cols] = piece
            else:
                long_out[k - 1 - nshort, 0:1, cols] = piece

    for c in range(chunks):
        to_cot(c).wait_send()

    @pl.when(has_up)
    def _():
        to_bot.wait_send()
        to_cbot.wait_send()
        for o in range(ndp):
            to_stat0(2, o, up_z).wait_send()

    @pl.when(has_down)
    def _():
        to_top.wait_send()
        for o in range(ndp):
            to_stat0(0, o, down_z).wait_send()

    for o in range(1, ndp):
        to_stat0(1, o, ctx).wait_send()
    for o in range(1, nctx):
        send_filters(0, o).wait_send()
        send_filters(1, o).wait_send()
        send_grads(o).wait_send()
    to_prev.wait_send()
    to_follow.wait_send()


def handed_on(a0, a1, a2, a3, b0, b1, b2, b3, sem):
    half = a0.shape[1] // 2
    pairs = [(a0.at[0, pl.ds(i * half, half), :], b0.at[0, pl.ds(i * half, half), :]) for i in range(2)]
    copies = [
        pltpu.make_async_copy(a, b, sem.at[i]) for i, (a, b) in enumerate(pairs + [(a1, b1), (a2, b2), (a3, b3)])
    ]
    for c in copies:
        c.start()
    for c in copies:
        c.wait()


def swap(values):
    return jnp.transpose(values, (1, 0, 2))


def per_device(mesh, hidden, cotangent, gain_rows, short_taps, long_taps):
    npipe, nctx, ndp = mesh.shape["pipe"], mesh.shape["ctx"], mesh.shape["dp"]
    nrow, chans = hidden.shape[1], hidden.shape[2]
    own = gain_rows.shape[1]
    wide = -(-own // LANES) * LANES
    nshort, nlong = short_taps.shape[1], long_taps.shape[1]
    ntap = 1 + nshort + nlong
    cb = wide // LANES
    nb = nctx * cb
    halo = 2 * (nshort // 3 + nlong - 2)
    total = nrow + 2 * halo
    slab_rows = -(-ntap * cb // 16) * 16
    ahead = next(n for n in (4, 2, 1) if nrow % (16 * n) == 0)
    chunks = next(n for n in (BACK, 1) if nrow % (16 * n) == 0)
    groups = nb // SUB
    nfwd = nshort // 3 - 1 + nlong - 1
    nbwd = nlong - 1 + 3 * (nshort // 3 - 1)

    def widen(values):
        if wide == own:
            return values
        lead = values.shape[:-1]
        blocks = values.reshape(lead + (-1, own))
        blocks = jnp.pad(blocks, [(0, 0)] * (len(lead) + 1) + [(0, wide - own)])
        return blocks.reshape(lead + (-1,))

    def narrow(values):
        if wide == own:
            return values
        lead = values.shape[:-1]
        return values.reshape(lead + (-1, wide))[..., :own].reshape(lead + (-1,))

    cfg = dict(
        npipe=npipe, nctx=nctx, ndp=ndp, nrow=nrow, nb=nb, cb=cb, ntap=ntap, nshort=nshort,
        width=float(chans * ndp), halo=halo, ahead=ahead, chunks=chunks,
    )
    full = nb * LANES
    dma = pltpu.SemaphoreType.DMA
    vmem = pl.BlockSpec(memory_space=pltpu.VMEM)
    anywhere = pl.BlockSpec(memory_space=pl.ANY)
    shapes = (
        jax.ShapeDtypeStruct((1, nrow, full), BF16),
        jax.ShapeDtypeStruct((1, wide), F32),
        jax.ShapeDtypeStruct((nshort, 1, wide), F32),
        jax.ShapeDtypeStruct((nlong, 1, wide), F32),
    )
    outs = pl.pallas_call(
        functools.partial(kernel, cfg),
        out_shape=tuple(pltpu.VMEM(s.shape, s.dtype) for s in shapes),
        in_specs=[anywhere, anywhere, vmem, vmem, vmem],
        out_specs=(vmem,) * 4,
        scratch_shapes=[
            pltpu.VMEM((nrow, full), BF16),
            pltpu.VMEM((halo, full), BF16),
            pltpu.VMEM((halo, full), BF16),
            pltpu.VMEM((nrow, full), BF16),
            pltpu.VMEM((halo, full), BF16),
            pltpu.VMEM((slab_rows, LANES), F32),
            pltpu.VMEM((2, nctx, slab_rows, LANES), F32),
            pltpu.VMEM((2, ntap * nb, LANES), F32),
            pltpu.VMEM((2, nshort * nb, LANES), F32),
            pltpu.VMEM((2, ntap * nb, LANES), F32),
            pltpu.VMEM((ntap * nb, LANES), F32),
            pltpu.VMEM((nctx, slab_rows, LANES), F32),
            pltpu.VMEM((nctx, slab_rows, LANES), BF16),
            pltpu.VMEM((nctx, slab_rows, LANES), BF16),
            pltpu.VMEM((total * nb, LANES), F32),
            pltpu.VMEM((total * nb, LANES), F32),
            pltpu.VMEM((total * nb, LANES), F32),
            pltpu.VMEM((total * nb, LANES), F32),
            pltpu.VMEM((total * nb, LANES), F32),
            pltpu.VMEM((2, 6, total * nb, LANES), F32),
            pltpu.VMEM((total * nb, LANES), F32),
            pltpu.VMEM((2 * groups * nfwd * SUB, LANES), F32),
            pltpu.VMEM((2 * groups * nbwd * SUB, LANES), F32),
            pltpu.VMEM((SUB, LANES), F32),
            pltpu.VMEM((3, ndp, SUB, LANES), F32),
            pltpu.VMEM((3, ahead, SUB, LANES), F32),
            pltpu.VMEM((3, ahead, ndp, SUB, LANES), F32),
            pltpu.VMEM((4, total, LANES), F32),
            dma((chunks,)),
            dma((3,)),
            dma((3,)),
            dma((chunks,)),
            dma((chunks,)),
            dma((2, nctx)),
            dma((2, nctx)),
            dma((1,)),
            dma((1,)),
            dma((nctx,)),
            dma((nctx,)),
            dma((3, ndp)),
            dma((3, ndp)),
            dma((3, ahead, ndp)),
            dma((3, ahead, ndp)),
        ],
        compiler_params=pltpu.CompilerParams(
            collective_id=0, has_side_effects=True, vmem_limit_bytes=62 * 1024 * 1024 - 1400 * 1024
        ),
        name="relay",
    )(widen(hidden), widen(cotangent), widen(gain_rows), swap(widen(short_taps)), swap(widen(long_taps)))
    outs = pl.pallas_call(
        handed_on,
        out_shape=shapes,
        in_specs=[vmem] * 4,
        out_specs=(anywhere,) * 4,
        scratch_shapes=[dma((5,))],
        compiler_params=pltpu.CompilerParams(vmem_limit_bytes=4 * 1024 * 1024),
        name="handed_on",
    )(*outs)
    return tuple(narrow(o) for o in (outs[0], outs[1], swap(outs[2]), swap(outs[3])))


def solution(mesh):
    in_specs = (
        P("pipe", "ctx", "dp"),
        P("pipe", "ctx", "dp"),
        P("pipe", ("dp", "ctx")),
        P("pipe", None, ("dp", "ctx")),
        P("pipe", None, ("dp", "ctx")),
    )
    out_specs = (
        P("pipe", "ctx", "dp"),
        P("pipe", ("dp", "ctx")),
        P("pipe", None, ("dp", "ctx")),
        P("pipe", None, ("dp", "ctx")),
    )
    return jax.shard_map(
        functools.partial(per_device, mesh), mesh=mesh, in_specs=in_specs, out_specs=out_specs, check_vma=False
    )
```

```python
import functools

import jax
import jax.numpy as jnp
from jax import lax
from jax.experimental import pallas as pl
from jax.experimental.pallas import tpu as pltpu
from jax.sharding import PartitionSpec as P

MESH = pl.DeviceIdType.MESH
F32 = jnp.float32
BF16 = jnp.bfloat16
LANES = 128
SUB = 8
EPS = 1e-05
BACK = 2


def kernel(
    cfg,
    hid,
    cot,
    gain_hbm,
    short_hbm,
    long_hbm,
    out,
    gain_out,
    short_out,
    long_out,
    gain_in,
    short_in,
    long_in,
    hbuf,
    htop,
    hbot,
    cbuf,
    cbot,
    slab,
    fr,
    filt,
    fold,
    grads,
    gin,
    gs,
    gsent,
    rg,
    xs,
    ys,
    zs,
    wd_outer,
    wd_inner,
    saved,
    parts,
    fstate,
    bstate,
    st0_send,
    st0_recv,
    st_send,
    st_recv,
    rows,
    in_sem,
    small_sem,
    halo_send,
    halo_recv,
    c_send,
    c_recv,
    f_send,
    f_recv,
    p_send,
    p_recv,
    g_send,
    g_recv,
    s0_send,
    s0_recv,
    s_send,
    s_recv,
):
    npipe, nctx, ndp = cfg["npipe"], cfg["nctx"], cfg["ndp"]
    nrow, nb, cb, ntap, nshort, width = (
        cfg["nrow"], cfg["nb"], cfg["cb"], cfg["ntap"], cfg["nshort"], cfg["width"],
    )
    ahead, chunks = cfg["ahead"], cfg["chunks"]
    taps = nshort // 3
    nlong = ntap - 1 - nshort
    halo = cfg["halo"]
    total = nrow + 2 * halo
    part = nrow // chunks
    groups = nb // SUB
    edge = halo // SUB
    slabs = SUB // cb if cb < SUB and SUB % cb == 0 else nctx
    slabs = min(slabs, nctx)
    teams = nctx // slabs
    nfwd = taps - 1 + nlong - 1
    nbwd = nlong - 1 + 3 * (taps - 1)
    pipe, ctx, dp = lax.axis_index("pipe"), lax.axis_index("ctx"), lax.axis_index("dp")
    prev = lax.rem(pipe + npipe - 1, npipe)
    follow = lax.rem(pipe + 1, npipe)

    def ctx_at(o):
        return lax.rem(ctx + o, nctx)

    def dp_at(o):
        return lax.rem(dp + o, ndp)

    def team_at(o):
        team = lax.rem(ctx // slabs + o // slabs, teams)
        return team * slabs + lax.rem(lax.rem(ctx, slabs) + o % slabs, slabs)

    def dev(p, z, d):
        return {"pipe": p, "ctx": z, "dp": d}

    def remote(src, dst, ss, rs, where):
        return pltpu.make_async_remote_copy(
            src_ref=src, dst_ref=dst, send_sem=ss, recv_sem=rs, device_id=where, device_id_type=MESH
        )

    barrier = pltpu.get_barrier_semaphore()
    peers = [(pipe, ctx_at(o), dp) for o in range(1, nctx)]
    for d in range(1, ndp):
        for o in sorted({0, 1 % nctx, (nctx - 1) % nctx}):
            peers.append((pipe, ctx_at(o), dp_at(d)))
    peers += [(prev, ctx, dp), (follow, ctx, dp), (follow, ctx_at(1), dp)]
    for p, z, d in peers:
        pl.semaphore_signal(barrier, inc=1, device_id=dev(p, z, d), device_id_type=MESH)

    def rows_of(c):
        return pl.ds(c * part, part)

    def load_hid(c):
        return pltpu.make_async_copy(hid.at[0, rows_of(c), :], hbuf.at[rows_of(c), :], in_sem.at[c])

    small = [
        pltpu.make_async_copy(a, b, small_sem.at[i])
        for i, (a, b) in enumerate(((gain_hbm, gain_in), (short_hbm, short_in), (long_hbm, long_in)))
    ]
    for copy in small:
        copy.start()
    for c in range(chunks):
        load_hid(c).start()

    zero = jnp.zeros((SUB, LANES), F32)
    for i in range(2 * groups * nfwd):
        fstate[i * SUB : (i + 1) * SUB, :] = zero
    for i in range(2 * groups * nbwd):
        bstate[i * SUB : (i + 1) * SUB, :] = zero
    for i in range(2 * ntap * groups):
        grads[i // (ntap * groups), i % (ntap * groups) * SUB : (i % (ntap * groups) + 1) * SUB, :] = zero

    lane = lax.broadcasted_iota(jnp.int32, (SUB, LANES), 1)

    def spread(dst, first, block):
        for half in range(2):
            piece = block[half * SUB : (half + 1) * SUB, :]
            start = (first + half * SUB) * SUB
            for j in range(nb):
                dst[pl.ds(j // SUB * total * SUB + start + j % SUB, SUB, stride=SUB), :] = piece[:, j * LANES : (j + 1) * LANES]

    def squares(stat, first, block):
        for half in range(2):
            acc = None
            for j in range(nb):
                piece = block[half * SUB : (half + 1) * SUB, j * LANES : (j + 1) * LANES]
                acc = piece * piece if acc is None else acc + piece * piece
            value = jnp.sum(acc, axis=1, keepdims=True)
            stat = jnp.where(lane == first // SUB + half, value, stat)
        return stat

    def take_hidden(i, stat):
        block = hbuf[pl.ds(pl.multiple_of(i * 16, 16), 16), :].astype(F32)
        spread(xs, halo + i * 16, block)
        return squares(stat, halo + i * 16, block)

    for copy in small:
        copy.wait()
    for k in range(ntap):
        src, row = (gain_in, 0) if k == 0 else ((short_in, k - 1) if k <= nshort else (long_in, k - 1 - nshort))
        for j in range(cb):
            cols = pl.ds(j * LANES, LANES)
            piece = src[row : row + 1, cols] if k == 0 else src[row, 0:1, cols]
            slab[k * cb + j : k * cb + j + 1, :] = piece
    pad = slab.shape[0] - ntap * cb
    if pad:
        slab[ntap * cb :, :] = jnp.zeros((pad, LANES), F32)
        for z in range(nctx):
            gs[z, ntap * cb :, :] = jnp.zeros((pad, LANES), F32)
    fr[0, ctx] = slab[...]
    stat = zero
    for c in range(chunks):
        load_hid(c).wait()
        stat = lax.fori_loop(c * part // 16, (c + 1) * part // 16, take_hidden, stat)
    st0_send[...] = stat
    st0_recv[1, dp] = stat

    pl.semaphore_wait(barrier, len(peers))

    up_z = lax.max(ctx - 1, 0)
    down_z = lax.min(ctx + 1, nctx - 1)
    head, tail = pl.ds(0, halo), pl.ds(nrow - halo, halo)
    to_bot = remote(hbuf.at[head, :], hbot, halo_send.at[0], halo_recv.at[0], dev(pipe, up_z, dp))
    to_top = remote(hbuf.at[tail, :], htop, halo_send.at[1], halo_recv.at[1], dev(pipe, down_z, dp))
    to_cbot = remote(cot.at[0, head, :], cbot, halo_send.at[2], halo_recv.at[2], dev(prev, up_z, dp))
    has_up, has_down = ctx > 0, ctx < nctx - 1

    def send_filters(b, o):
        mine = fr.at[1, ctx] if b else slab
        return remote(mine, fr.at[b, ctx], f_send.at[b, o], f_recv.at[b, ctx], dev(pipe, team_at(o), dp))

    def wait_filters(b, o):
        there = team_at(o)
        remote(slab, fr.at[b, there], f_send.at[b, o], f_recv.at[b, there], dev(pipe, there, dp)).wait_recv()

    to_prev = remote(slab, fr.at[1, ctx], f_send.at[1, 0], f_recv.at[1, ctx], dev(prev, ctx, dp))

    def to_stat0(slot, o, z):
        return remote(st0_send, st0_recv.at[slot, dp], s0_send.at[slot, o], s0_recv.at[slot, dp], dev(pipe, z, dp_at(o)))

    def from_stat0(slot, o, z):
        there = dp_at(o)
        return remote(
            st0_send, st0_recv.at[slot, there], s0_send.at[slot, o], s0_recv.at[slot, there], dev(pipe, z, there)
        )

    for o in range(1, nctx):
        send_filters(0, o).start()

    @pl.when(has_down)
    def _():
        to_top.start()
        for o in range(ndp):
            to_stat0(0, o, down_z).start()

    for o in range(1, ndp):
        to_stat0(1, o, ctx).start()

    @pl.when(has_up)
    def _():
        to_bot.start()
        for o in range(ndp):
            to_stat0(2, o, up_z).start()
        to_cbot.start()

    def to_cot(c):
        return remote(
            cot.at[0, rows_of(c), :], cbuf.at[rows_of(c), :], c_send.at[c], c_recv.at[c], dev(prev, ctx, dp)
        )

    to_prev.start()
    for c in range(chunks - 1, -1, -1):
        to_cot(c).start()

    @pl.when(has_up)
    def _():
        remote(htop, htop, halo_send.at[1], halo_recv.at[1], dev(pipe, up_z, dp)).wait_recv()
        for o in range(ndp):
            from_stat0(0, o, up_z).wait_recv()

    @pl.when(jnp.logical_not(has_up))
    def _():
        htop[...] = jnp.zeros(htop.shape, BF16)
        for d in range(ndp):
            st0_recv[0, d] = zero

    @pl.when(has_down)
    def _():
        remote(hbot, hbot, halo_send.at[0], halo_recv.at[0], dev(pipe, down_z, dp)).wait_recv()
        for o in range(ndp):
            from_stat0(2, o, down_z).wait_recv()

    @pl.when(jnp.logical_not(has_down))
    def _():
        hbot[...] = jnp.zeros(hbot.shape, BF16)
        for d in range(ndp):
            st0_recv[2, d] = zero

    remote(slab, fr.at[1, ctx], f_send.at[1, 0], f_recv.at[1, ctx], dev(follow, ctx, dp)).wait_recv()
    for o in range(1, nctx):
        send_filters(1, o).start()

    spread(xs, 0, htop[...].astype(F32))
    spread(xs, halo + nrow, hbot[...].astype(F32))

    def row_scale(value):
        return lax.rsqrt(value / width + EPS)

    def mean_of(value):
        return value / width

    def put_rows(stage, at_octet, value, i):
        column = jnp.sum(jnp.where(lane == i, value, 0.0), axis=1, keepdims=True)
        rows[stage, pl.ds(pl.multiple_of(at_octet * SUB, SUB), SUB), :] = jnp.broadcast_to(column, (SUB, LANES))

    for o in range(1, ndp):
        from_stat0(1, o, ctx).wait_recv()
    sums = []
    for slot in range(3):
        value = st0_recv[slot, 0]
        for d in range(1, ndp):
            value = value + st0_recv[slot, d]
        sums.append(row_scale(value))
    for i in range(edge):
        put_rows(0, i, sums[0], i + nrow // SUB)
        put_rows(0, edge + nrow // SUB + i, sums[2], i + edge)
    for i in range(edge, edge + nrow // SUB):
        put_rows(0, i, sums[1], i)

    def first_octet(many, c):
        return jnp.where(c == 0, 0, edge + nrow // SUB // many * c)

    def span(many):
        return nrow // SUB // many + edge

    def send_stat(stage, c, value):
        st_send[stage, c] = value
        st_recv[stage, c, dp] = value
        for o in range(1, ndp):
            remote(
                st_send.at[stage, c], st_recv.at[stage, c, dp], s_send.at[stage, c, o], s_recv.at[stage, c, dp],
                dev(pipe, ctx, dp_at(o)),
            ).start()

    def get_stat(stage, many, c, fn):
        for o in range(1, ndp):
            there = dp_at(o)
            remote(
                st_send.at[stage, c], st_recv.at[stage, c, there], s_send.at[stage, c, o], s_recv.at[stage, c, there],
                dev(pipe, ctx, there),
            ).wait()
        value = st_recv[stage, c, 0]
        for d in range(1, ndp):
            value = value + st_recv[stage, c, d]
        value = fn(value)
        base = first_octet(many, c)
        for k in range(span(many)):
            put_rows(stage + 1, base + k, value, base + k)

    def collect(many, c):
        base = first_octet(many, c)
        value = zero
        for n in range(span(many)):
            acc = None
            for k in range(SUB):
                piece = parts[pl.ds((base + n) * SUB * SUB + k, SUB, stride=SUB), :]
                acc = piece if acc is None else acc + piece
            value = jnp.where(lane == base + n, jnp.sum(acc, axis=1, keepdims=True), value)
        return value

    per = groups // teams

    def spot(k, g):
        return pl.ds(k * nb + g * SUB if isinstance(g, int) else pl.multiple_of(k * nb + g * SUB, SUB), SUB)

    def build_filters(b, team):
        for n in range(per):
            g = team * per + n
            first = n * SUB // cb
            many = max(SUB // cb, 1)
            for k in range(ntap):
                if cb >= SUB:
                    z, row = n * SUB // cb, n * SUB % cb
                    value = fr[b, team * slabs + z, k * cb + row : k * cb + row + SUB, :]
                else:
                    value = jnp.concatenate(
                        [fr[b, team * slabs + first + s, k * cb : (k + 1) * cb, :] for s in range(many)], axis=0
                    )
                filt[b, spot(k, g), :] = value
                if k == 0:
                    gain = value
                elif k <= nshort:
                    fold[b, spot(k - 1, g), :] = value * gain

    def at(w, g):
        return pl.ds(pl.multiple_of((g * total + w) * SUB, SUB), SUB)

    def row_of(stage, w):
        return jnp.broadcast_to(rows[stage, pl.ds(w, 1), :], (SUB, LANES))

    def kept(ref, b, g, count, i):
        return ref.at[pl.ds(((b * groups + g) * count + i) * SUB, SUB), :]

    def add_part(w, g, value):
        here = at(w, 0)
        parts[here, :] = value if g == 0 else parts[here, :] + value

    def forward(b, c, start, unroll):
        part, chunks = nrow // ahead, ahead
        lo = jnp.where(c == 0, start, halo + part * c)
        hi = jnp.where(c == chunks - 1, total, halo + part * (c + 1))

        def step(it, _):
            for g in range(groups):
                short = [fold[b, spot(k, g), :] for k in range(nshort)]
                long = [filt[b, spot(1 + nshort + k, g), :] for k in range(nlong)]
                held = [kept(fstate, b, g, nfwd, i) for i in range(nfwd)]
                lag = [ref[...] for ref in held[: taps - 1]]
                past = [ref[...] for ref in held[taps - 1 :]]
                for u in range(unroll):
                    w = lo + it * unroll + u
                    x = (xs if b == 0 else ys)[at(w, g), :]
                    xh = x * row_of(b, w)
                    seq = [xh] + lag
                    streams = []
                    for j in range(3):
                        value = short[taps * j] * seq[0]
                        for i in range(1, taps):
                            value = value + short[taps * j + i] * seq[i]
                        streams.append(value)
                    products = [streams[1] * streams[2]] + past
                    mix = long[0] * products[0]
                    for i in range(1, nlong):
                        mix = mix + long[i] * products[i]
                    for n, value in enumerate((xh, streams[0], streams[1], streams[2], mix, products[0])):
                        saved[b, n, at(w, g), :] = value
                    if b == 0:
                        inner = (x + streams[0] * mix).astype(BF16).astype(F32)
                        ys[at(w, g), :] = inner
                        add_part(w, g, inner * inner)
                    lag, past = seq[:-1], products[:-1]
                for ref, value in zip(held, lag + past):
                    ref[...] = value
            return 0

        lax.fori_loop(0, (hi - lo) // unroll, step, 0)

    for o in range(1, nctx):
        wait_filters(0, o)
    for n in range(teams):
        build_filters(0, n)

    def ahead_inner(c, _):
        forward(0, c, 0, 16)
        send_stat(0, c, collect(ahead, c))
        return 0

    lax.fori_loop(0, ahead, ahead_inner, 0)

    for o in range(1, nctx):
        wait_filters(1, o)
    for n in range(teams):
        build_filters(1, n)

    def ahead_outer(c, _):
        get_stat(0, ahead, c, row_scale)
        forward(1, c, 0, 16)
        return 0

    lax.fori_loop(0, ahead, ahead_outer, 0)

    @pl.when(has_down)
    def _():
        remote(cbot, cbot, halo_send.at[2], halo_recv.at[2], dev(follow, down_z, dp)).wait_recv()

    @pl.when(jnp.logical_not(has_down))
    def _():
        cbot[...] = jnp.zeros(cbot.shape, BF16)

    spread(zs, halo + nrow, cbot[...].astype(F32))

    def take_cot(i, _):
        spread(zs, halo + i * 16, cbuf[pl.ds(pl.multiple_of(i * 16, 16), 16), :].astype(F32))
        return 0

    def backward(b, c, top, brief, unroll):
        lo = halo + part * c
        hi = lo + part

        def one(g, w, short, long, state, acc):
            dmix_next, ds_next = state
            here = at(w, g)
            up = zs[here, :]
            if b == 0:
                up = up + row_of(1, w) * (wd_outer[here, :] - saved[1, 0, here, :] * row_of(2, w))
                xs[here, :] = up
            xh, query, key, value, mix, product = [saved[b, n, here, :] for n in range(6)]
            dmix = [up * query] + dmix_next
            dprod = long[0] * dmix[0]
            for i in range(1, nlong):
                dprod = dprod + long[i] * dmix[i]
            ds = [[up * mix] + ds_next[0], [dprod * value] + ds_next[1], [dprod * key] + ds_next[2]]
            weighted = None
            for j in range(3):
                for i in range(taps):
                    term = short[taps * j + i] * ds[j][i]
                    weighted = term if weighted is None else weighted + term
            (wd_outer if b == 1 else wd_inner)[here, :] = weighted
            add_part(w, g, xh * weighted)
            if acc is not None:
                fresh = []
                for j in range(3):
                    for i in range(taps):
                        fresh.append(acc[taps * j + i] + xh * ds[j][i])
                for i in range(nlong):
                    fresh.append(acc[nshort + i] + product * dmix[i])
                acc = fresh
            return (dmix[:-1], [d[:-1] for d in ds]), acc

        def flat(state):
            return list(state[0]) + [v for d in state[1] for v in d]

        def unflat(vals):
            n = nlong - 1
            rest = vals[n:]
            m = taps - 1
            return list(vals[:n]), [list(rest[j * m : (j + 1) * m]) for j in range(3)]

        def rows_back(high, many, summed):
            def step(it, _):
                for g in range(groups):
                    short = [fold[b, spot(k, g), :] for k in range(nshort)]
                    long = [filt[b, spot(1 + nshort + k, g), :] for k in range(nlong)]
                    held = [kept(bstate, b, g, nbwd, i) for i in range(nbwd)]
                    state = unflat([ref[...] for ref in held])
                    acc = [grads[b, spot(k, g), :] for k in range(1, ntap)] if summed else None
                    for u in range(many):
                        state, acc = one(g, high - 1 - it * many - u, short, long, state, acc)
                    for ref, value in zip(held, flat(state)):
                        ref[...] = value
                    if summed:
                        for k in range(1, ntap):
                            grads[b, spot(k, g), :] = acc[k - 1]
                return 0

            return step

        extra = jnp.where(c == chunks - 1, (top - halo - nrow) // brief, 0)
        lax.fori_loop(0, extra, rows_back(top, brief, False), 0)
        lax.fori_loop(0, part // unroll, rows_back(hi, unroll, True), 0)

    def back_outer(it, _):
        c = chunks - 1 - it
        remote(
            cbuf.at[rows_of(c), :], cbuf.at[rows_of(c), :], c_send.at[c], c_recv.at[c], dev(follow, ctx, dp)
        ).wait_recv()
        lax.fori_loop(c * (part // 16), (c + 1) * (part // 16), take_cot, 0)
        backward(1, c, total, 8, 16)
        send_stat(1, c, collect(chunks, c))
        return 0

    lax.fori_loop(0, chunks, back_outer, 0)

    def finish_grads(b):
        for g in range(groups):
            gain = filt[b, spot(0, g), :]
            acc = None
            for k in range(1, 1 + nshort):
                raw = grads[b, spot(k, g), :]
                term = raw * filt[b, spot(k, g), :]
                acc = term if acc is None else acc + term
                grads[b, spot(k, g), :] = raw * gain
            grads[b, spot(0, g), :] = acc

    finish_grads(1)
    to_follow = remote(grads.at[1], gin, p_send.at[0], p_recv.at[0], dev(follow, ctx, dp))
    to_follow.start()

    def send_grads(o):
        z = ctx_at(o)
        return remote(gsent.at[z], rg.at[ctx], g_send.at[o], g_recv.at[ctx], dev(pipe, z, dp))

    def share_grads():
        finish_grads(0)
        remote(grads.at[1], gin, p_send.at[0], p_recv.at[0], dev(prev, ctx, dp)).wait_recv()
        for z in range(nctx):
            for k in range(ntap):
                here = pl.ds(k * nb + z * cb, cb)
                gs[z, k * cb : (k + 1) * cb, :] = grads[0, here, :] + gin[here, :]
            gsent[z] = gs[z].astype(BF16)
        for o in range(1, nctx):
            send_grads(o).start()

    def back_inner(it, _):
        c = chunks - 1 - it
        get_stat(1, chunks, c, mean_of)
        backward(0, c, halo + nrow + halo // 2, 8, 16)

        @pl.when(c == 0)
        def _():
            share_grads()

        send_stat(2, c, collect(chunks, c))
        return 0

    lax.fori_loop(0, chunks, back_inner, 0)

    def finish(i, _):
        w = halo + i * 16
        halves = [pl.multiple_of(w + half * SUB, SUB) for half in range(2)]
        scales = [rows[0, pl.ds(h, SUB), :] for h in halves]
        means = [rows[3, pl.ds(h, SUB), :] for h in halves]
        for j in range(nb):
            pieces = []
            for half in range(2):
                here = pl.ds(j // SUB * total * SUB + halves[half] * SUB + j % SUB, SUB, stride=SUB)
                pieces.append(xs[here, :] + scales[half] * (wd_inner[here, :] - saved[0, 0, here, :] * means[half]))
            out[0, pl.ds(pl.multiple_of(i * 16, 16), 16), j * LANES : (j + 1) * LANES] = jnp.concatenate(
                pieces, axis=0
            ).astype(BF16)
        return 0

    def wind_up(it, _):
        c = chunks - 1 - it
        get_stat(2, chunks, c, mean_of)
        lax.fori_loop(c * (part // 16), (c + 1) * (part // 16), finish, 0)
        return 0

    lax.fori_loop(0, chunks, wind_up, 0)

    for c in range(chunks):
        to_cot(c).wait_send()

    @pl.when(has_up)
    def _():
        to_bot.wait_send()
        to_cbot.wait_send()
        for o in range(ndp):
            to_stat0(2, o, up_z).wait_send()

    @pl.when(has_down)
    def _():
        to_top.wait_send()
        for o in range(ndp):
            to_stat0(0, o, down_z).wait_send()

    for o in range(1, ndp):
        to_stat0(1, o, ctx).wait_send()
    for o in range(1, nctx):
        send_filters(0, o).wait_send()
        send_filters(1, o).wait_send()
    to_prev.wait_send()
    to_follow.wait_send()

    for o in range(1, nctx):
        z = ctx_at(o)
        remote(gsent.at[z], rg.at[z], g_send.at[o], g_recv.at[z], dev(pipe, z, dp)).wait_recv()
    result = gs[ctx]
    for o in range(1, nctx):
        result = result + rg[ctx_at(o)].astype(F32)
    for k in range(ntap):
        for j in range(cb):
            cols = pl.ds(j * LANES, LANES)
            piece = result[k * cb + j : k * cb + j + 1, :]
            if k == 0:
                gain_out[0:1, cols] = piece
            elif k <= nshort:
                short_out[k - 1, 0:1, cols] = piece
            else:
                long_out[k - 1 - nshort, 0:1, cols] = piece

    for o in range(1, nctx):
        send_grads(o).wait_send()


def handed_on(a0, a1, a2, a3, b0, b1, b2, b3, sem):
    half = a0.shape[1] // 2
    pairs = [(a0.at[0, pl.ds(i * half, half), :], b0.at[0, pl.ds(i * half, half), :]) for i in range(2)]
    copies = [
        pltpu.make_async_copy(a, b, sem.at[i]) for i, (a, b) in enumerate(pairs + [(a1, b1), (a2, b2), (a3, b3)])
    ]
    for c in copies:
        c.start()
    for c in copies:
        c.wait()


def swap(values):
    return jnp.transpose(values, (1, 0, 2))


def per_device(mesh, hidden, cotangent, gain_rows, short_taps, long_taps):
    npipe, nctx, ndp = mesh.shape["pipe"], mesh.shape["ctx"], mesh.shape["dp"]
    nrow, chans = hidden.shape[1], hidden.shape[2]
    own = gain_rows.shape[1]
    wide = -(-own // LANES) * LANES
    nshort, nlong = short_taps.shape[1], long_taps.shape[1]
    ntap = 1 + nshort + nlong
    cb = wide // LANES
    nb = nctx * cb
    halo = 2 * (nshort // 3 + nlong - 2)
    total = nrow + 2 * halo
    slab_rows = -(-ntap * cb // 16) * 16
    ahead = next(n for n in (4, 2, 1) if nrow % (16 * n) == 0)
    chunks = next(n for n in (BACK, 1) if nrow % (16 * n) == 0)
    groups = nb // SUB
    nfwd = nshort // 3 - 1 + nlong - 1
    nbwd = nlong - 1 + 3 * (nshort // 3 - 1)

    def widen(values):
        if wide == own:
            return values
        lead = values.shape[:-1]
        blocks = values.reshape(lead + (-1, own))
        blocks = jnp.pad(blocks, [(0, 0)] * (len(lead) + 1) + [(0, wide - own)])
        return blocks.reshape(lead + (-1,))

    def narrow(values):
        if wide == own:
            return values
        lead = values.shape[:-1]
        return values.reshape(lead + (-1, wide))[..., :own].reshape(lead + (-1,))

    cfg = dict(
        npipe=npipe, nctx=nctx, ndp=ndp, nrow=nrow, nb=nb, cb=cb, ntap=ntap, nshort=nshort,
        width=float(chans * ndp), halo=halo, ahead=ahead, chunks=chunks,
    )
    full = nb * LANES
    dma = pltpu.SemaphoreType.DMA
    vmem = pl.BlockSpec(memory_space=pltpu.VMEM)
    anywhere = pl.BlockSpec(memory_space=pl.ANY)
    shapes = (
        jax.ShapeDtypeStruct((1, nrow, full), BF16),
        jax.ShapeDtypeStruct((1, wide), F32),
        jax.ShapeDtypeStruct((nshort, 1, wide), F32),
        jax.ShapeDtypeStruct((nlong, 1, wide), F32),
    )
    outs = pl.pallas_call(
        functools.partial(kernel, cfg),
        out_shape=tuple(pltpu.VMEM(s.shape, s.dtype) for s in shapes),
        in_specs=[anywhere] * 5,
        out_specs=(vmem,) * 4,
        scratch_shapes=[
            pltpu.VMEM((1, wide), F32),
            pltpu.VMEM((nshort, 1, wide), F32),
            pltpu.VMEM((nlong, 1, wide), F32),
            pltpu.VMEM((nrow, full), BF16),
            pltpu.VMEM((halo, full), BF16),
            pltpu.VMEM((halo, full), BF16),
            pltpu.VMEM((nrow, full), BF16),
            pltpu.VMEM((halo, full), BF16),
            pltpu.VMEM((slab_rows, LANES), F32),
            pltpu.VMEM((2, nctx, slab_rows, LANES), F32),
            pltpu.VMEM((2, ntap * nb, LANES), F32),
            pltpu.VMEM((2, nshort * nb, LANES), F32),
            pltpu.VMEM((2, ntap * nb, LANES), F32),
            pltpu.VMEM((ntap * nb, LANES), F32),
            pltpu.VMEM((nctx, slab_rows, LANES), F32),
            pltpu.VMEM((nctx, slab_rows, LANES), BF16),
            pltpu.VMEM((nctx, slab_rows, LANES), BF16),
            pltpu.VMEM((total * nb, LANES), F32),
            pltpu.VMEM((total * nb, LANES), F32),
            pltpu.VMEM((total * nb, LANES), F32),
            pltpu.VMEM((total * nb, LANES), F32),
            pltpu.VMEM((total * nb, LANES), F32),
            pltpu.VMEM((2, 6, total * nb, LANES), F32),
            pltpu.VMEM((total * SUB, LANES), F32),
            pltpu.VMEM((2 * groups * nfwd * SUB, LANES), F32),
            pltpu.VMEM((2 * groups * nbwd * SUB, LANES), F32),
            pltpu.VMEM((SUB, LANES), F32),
            pltpu.VMEM((3, ndp, SUB, LANES), F32),
            pltpu.VMEM((3, ahead, SUB, LANES), F32),
            pltpu.VMEM((3, ahead, ndp, SUB, LANES), F32),
            pltpu.VMEM((4, total, LANES), F32),
            dma((chunks,)),
            dma((3,)),
            dma((3,)),
            dma((3,)),
            dma((chunks,)),
            dma((chunks,)),
            dma((2, nctx)),
            dma((2, nctx)),
            dma((1,)),
            dma((1,)),
            dma((nctx,)),
            dma((nctx,)),
            dma((3, ndp)),
            dma((3, ndp)),
            dma((3, ahead, ndp)),
            dma((3, ahead, ndp)),
        ],
        compiler_params=pltpu.CompilerParams(
            collective_id=0, has_side_effects=True, vmem_limit_bytes=62 * 1024 * 1024 - 1400 * 1024
        ),
        name="relay",
    )(widen(hidden), widen(cotangent), widen(gain_rows), swap(widen(short_taps)), swap(widen(long_taps)))
    outs = pl.pallas_call(
        handed_on,
        out_shape=shapes,
        in_specs=[vmem] * 4,
        out_specs=(anywhere,) * 4,
        scratch_shapes=[dma((5,))],
        compiler_params=pltpu.CompilerParams(vmem_limit_bytes=4 * 1024 * 1024),
        name="handed_on",
    )(*outs)
    return tuple(narrow(o) for o in (outs[0], outs[1], swap(outs[2]), swap(outs[3])))


def solution(mesh):
    in_specs = (
        P("pipe", "ctx", "dp"),
        P("pipe", "ctx", "dp"),
        P("pipe", ("dp", "ctx")),
        P("pipe", None, ("dp", "ctx")),
        P("pipe", None, ("dp", "ctx")),
    )
    out_specs = (
        P("pipe", "ctx", "dp"),
        P("pipe", ("dp", "ctx")),
        P("pipe", None, ("dp", "ctx")),
        P("pipe", None, ("dp", "ctx")),
    )
    return jax.shard_map(
        functools.partial(per_device, mesh), mesh=mesh, in_specs=in_specs, out_specs=out_specs, check_vma=False
    )
```

```python
import functools

import jax
import jax.numpy as jnp
from jax import lax
from jax.experimental import pallas as pl
from jax.experimental.pallas import tpu as pltpu
from jax.sharding import PartitionSpec as P

MESH = pl.DeviceIdType.MESH
F32 = jnp.float32
BF16 = jnp.bfloat16
LANES = 128
SUB = 8
EPS = 1e-05
BACK = 2


def kernel(
    cfg,
    hid,
    cot,
    gain_hbm,
    short_hbm,
    long_hbm,
    out,
    gain_out,
    short_out,
    long_out,
    gain_in,
    short_in,
    long_in,
    hbuf,
    htop,
    hbot,
    cbuf,
    cbot,
    slab,
    fr,
    filt,
    fold,
    grads,
    gin,
    gs,
    gsent,
    rg,
    xs,
    ys,
    zs,
    wd_outer,
    wd_inner,
    saved,
    parts,
    fstate,
    bstate,
    st0_send,
    st0_recv,
    st_send,
    st_recv,
    rows,
    in_sem,
    small_sem,
    halo_send,
    halo_recv,
    c_send,
    c_recv,
    f_send,
    f_recv,
    p_send,
    p_recv,
    g_send,
    g_recv,
    s0_send,
    s0_recv,
    s_send,
    s_recv,
):
    npipe, nctx, ndp = cfg["npipe"], cfg["nctx"], cfg["ndp"]
    nrow, nb, cb, ntap, nshort, width = (
        cfg["nrow"], cfg["nb"], cfg["cb"], cfg["ntap"], cfg["nshort"], cfg["width"],
    )
    ahead, chunks = cfg["ahead"], cfg["chunks"]
    taps = nshort // 3
    nlong = ntap - 1 - nshort
    halo = cfg["halo"]
    total = nrow + 2 * halo
    part = nrow // chunks
    reach = nrow // ahead + (halo if ahead == 2 else 2 * halo)
    ahead_rows = next(n for n in (24, 16, 8) if reach % n == 0)
    back_rows = next(n for n in (32, 16) if part % n == 0)
    groups = nb // SUB
    edge = halo // SUB
    slabs = SUB // cb if cb < SUB and SUB % cb == 0 else nctx
    slabs = min(slabs, nctx)
    teams = nctx // slabs
    nfwd = taps - 1 + nlong - 1
    nbwd = nlong - 1 + 3 * (taps - 1)
    pipe, ctx, dp = lax.axis_index("pipe"), lax.axis_index("ctx"), lax.axis_index("dp")
    prev = lax.rem(pipe + npipe - 1, npipe)
    follow = lax.rem(pipe + 1, npipe)

    def ctx_at(o):
        return lax.rem(ctx + o, nctx)

    def dp_at(o):
        return lax.rem(dp + o, ndp)

    def team_at(o):
        team = lax.rem(ctx // slabs + o // slabs, teams)
        return team * slabs + lax.rem(lax.rem(ctx, slabs) + o % slabs, slabs)

    def dev(p, z, d):
        return {"pipe": p, "ctx": z, "dp": d}

    def remote(src, dst, ss, rs, where):
        return pltpu.make_async_remote_copy(
            src_ref=src, dst_ref=dst, send_sem=ss, recv_sem=rs, device_id=where, device_id_type=MESH
        )

    barrier = pltpu.get_barrier_semaphore()
    peers = [(pipe, ctx_at(o), dp) for o in range(1, nctx)]
    for d in range(1, ndp):
        for o in sorted({0, 1 % nctx, (nctx - 1) % nctx}):
            peers.append((pipe, ctx_at(o), dp_at(d)))
    peers += [(prev, ctx, dp), (follow, ctx, dp), (follow, ctx_at(1), dp)]
    for p, z, d in peers:
        pl.semaphore_signal(barrier, inc=1, device_id=dev(p, z, d), device_id_type=MESH)

    def rows_of(c):
        return pl.ds(c * part, part)

    def load_hid(c):
        return pltpu.make_async_copy(hid.at[0, rows_of(c), :], hbuf.at[rows_of(c), :], in_sem.at[c])

    small = [
        pltpu.make_async_copy(a, b, small_sem.at[i])
        for i, (a, b) in enumerate(((gain_hbm, gain_in), (short_hbm, short_in), (long_hbm, long_in)))
    ]
    for copy in small:
        copy.start()
    for c in range(chunks):
        load_hid(c).start()

    zero = jnp.zeros((SUB, LANES), F32)
    for i in range(2 * groups * nfwd):
        fstate[i * SUB : (i + 1) * SUB, :] = zero
    for i in range(2 * groups * nbwd):
        bstate[i * SUB : (i + 1) * SUB, :] = zero
    for i in range(2 * ntap * groups):
        grads[i // (ntap * groups), i % (ntap * groups) * SUB : (i % (ntap * groups) + 1) * SUB, :] = zero

    lane = lax.broadcasted_iota(jnp.int32, (SUB, LANES), 1)

    def spread(dst, first, block):
        for half in range(2):
            piece = block[half * SUB : (half + 1) * SUB, :]
            start = (first + half * SUB) * SUB
            for j in range(nb):
                dst[pl.ds(j // SUB * total * SUB + start + j % SUB, SUB, stride=SUB), :] = piece[:, j * LANES : (j + 1) * LANES]

    def squares(stat, first, block):
        for half in range(2):
            acc = None
            for j in range(nb):
                piece = block[half * SUB : (half + 1) * SUB, j * LANES : (j + 1) * LANES]
                acc = piece * piece if acc is None else acc + piece * piece
            value = jnp.sum(acc, axis=1, keepdims=True)
            stat = jnp.where(lane == first // SUB + half, value, stat)
        return stat

    def take_hidden(i, stat):
        block = hbuf[pl.ds(pl.multiple_of(i * 16, 16), 16), :].astype(F32)
        spread(xs, halo + i * 16, block)
        return squares(stat, halo + i * 16, block)

    for copy in small:
        copy.wait()
    for k in range(ntap):
        src, row = (gain_in, 0) if k == 0 else ((short_in, k - 1) if k <= nshort else (long_in, k - 1 - nshort))
        for j in range(cb):
            cols = pl.ds(j * LANES, LANES)
            piece = src[row : row + 1, cols] if k == 0 else src[row, 0:1, cols]
            slab[k * cb + j : k * cb + j + 1, :] = piece
    pad = slab.shape[0] - ntap * cb
    if pad:
        slab[ntap * cb :, :] = jnp.zeros((pad, LANES), F32)
        for z in range(nctx):
            gs[z, ntap * cb :, :] = jnp.zeros((pad, LANES), F32)
    fr[0, ctx] = slab[...]
    stat = zero
    for c in range(chunks):
        load_hid(c).wait()
        stat = lax.fori_loop(c * part // 16, (c + 1) * part // 16, take_hidden, stat)
    st0_send[...] = stat
    st0_recv[1, dp] = stat

    pl.semaphore_wait(barrier, len(peers))

    up_z = lax.max(ctx - 1, 0)
    down_z = lax.min(ctx + 1, nctx - 1)
    head, tail = pl.ds(0, halo), pl.ds(nrow - halo, halo)
    to_bot = remote(hbuf.at[head, :], hbot, halo_send.at[0], halo_recv.at[0], dev(pipe, up_z, dp))
    to_top = remote(hbuf.at[tail, :], htop, halo_send.at[1], halo_recv.at[1], dev(pipe, down_z, dp))
    to_cbot = remote(cot.at[0, head, :], cbot, halo_send.at[2], halo_recv.at[2], dev(prev, up_z, dp))
    has_up, has_down = ctx > 0, ctx < nctx - 1

    def send_filters(b, o):
        mine = fr.at[1, ctx] if b else slab
        return remote(mine, fr.at[b, ctx], f_send.at[b, o], f_recv.at[b, ctx], dev(pipe, team_at(o), dp))

    def wait_filters(b, o):
        there = team_at(o)
        remote(slab, fr.at[b, there], f_send.at[b, o], f_recv.at[b, there], dev(pipe, there, dp)).wait_recv()

    to_prev = remote(slab, fr.at[1, ctx], f_send.at[1, 0], f_recv.at[1, ctx], dev(prev, ctx, dp))

    def to_stat0(slot, o, z):
        return remote(st0_send, st0_recv.at[slot, dp], s0_send.at[slot, o], s0_recv.at[slot, dp], dev(pipe, z, dp_at(o)))

    def from_stat0(slot, o, z):
        there = dp_at(o)
        return remote(
            st0_send, st0_recv.at[slot, there], s0_send.at[slot, o], s0_recv.at[slot, there], dev(pipe, z, there)
        )

    for o in range(1, ndp):
        to_stat0(1, o, ctx).start()

    @pl.when(has_down)
    def _():
        for o in range(ndp):
            to_stat0(0, o, down_z).start()

    @pl.when(has_up)
    def _():
        for o in range(ndp):
            to_stat0(2, o, up_z).start()

    for o in range(nctx - 1, 1, -1):
        send_filters(0, o).start()

    @pl.when(has_down)
    def _():
        to_top.start()

    send_filters(0, 1).start()

    @pl.when(has_up)
    def _():
        to_bot.start()
        to_cbot.start()

    def to_cot(c):
        return remote(
            cot.at[0, rows_of(c), :], cbuf.at[rows_of(c), :], c_send.at[c], c_recv.at[c], dev(prev, ctx, dp)
        )

    to_prev.start()
    for c in range(chunks - 1, -1, -1):
        to_cot(c).start()

    @pl.when(has_up)
    def _():
        remote(htop, htop, halo_send.at[1], halo_recv.at[1], dev(pipe, up_z, dp)).wait_recv()
        for o in range(ndp):
            from_stat0(0, o, up_z).wait_recv()

    @pl.when(jnp.logical_not(has_up))
    def _():
        htop[...] = jnp.zeros(htop.shape, BF16)
        for d in range(ndp):
            st0_recv[0, d] = zero

    @pl.when(has_down)
    def _():
        remote(hbot, hbot, halo_send.at[0], halo_recv.at[0], dev(pipe, down_z, dp)).wait_recv()
        for o in range(ndp):
            from_stat0(2, o, down_z).wait_recv()

    @pl.when(jnp.logical_not(has_down))
    def _():
        hbot[...] = jnp.zeros(hbot.shape, BF16)
        for d in range(ndp):
            st0_recv[2, d] = zero

    remote(slab, fr.at[1, ctx], f_send.at[1, 0], f_recv.at[1, ctx], dev(follow, ctx, dp)).wait_recv()
    for o in range(1, nctx):
        send_filters(1, o).start()

    spread(xs, 0, htop[...].astype(F32))
    spread(xs, halo + nrow, hbot[...].astype(F32))

    def row_scale(value):
        return lax.rsqrt(value / width + EPS)

    def mean_of(value):
        return value / width

    def put_rows(stage, at_octet, value, i):
        column = jnp.sum(jnp.where(lane == i, value, 0.0), axis=1, keepdims=True)
        rows[stage, pl.ds(pl.multiple_of(at_octet * SUB, SUB), SUB), :] = jnp.broadcast_to(column, (SUB, LANES))

    for o in range(1, ndp):
        from_stat0(1, o, ctx).wait_recv()
    sums = []
    for slot in range(3):
        value = st0_recv[slot, 0]
        for d in range(1, ndp):
            value = value + st0_recv[slot, d]
        sums.append(row_scale(value))
    for i in range(edge):
        put_rows(0, i, sums[0], i + nrow // SUB)
        put_rows(0, edge + nrow // SUB + i, sums[2], i + edge)
    for i in range(edge, edge + nrow // SUB):
        put_rows(0, i, sums[1], i)

    def first_octet(many, c):
        return jnp.where(c == 0, 0, edge + nrow // SUB // many * c)

    def span(many):
        return nrow // SUB // many + edge

    def send_stat(stage, c, value):
        st_send[stage, c] = value
        st_recv[stage, c, dp] = value
        for o in range(1, ndp):
            remote(
                st_send.at[stage, c], st_recv.at[stage, c, dp], s_send.at[stage, c, o], s_recv.at[stage, c, dp],
                dev(pipe, ctx, dp_at(o)),
            ).start()

    def get_stat(stage, many, c, fn):
        for o in range(1, ndp):
            there = dp_at(o)
            remote(
                st_send.at[stage, c], st_recv.at[stage, c, there], s_send.at[stage, c, o], s_recv.at[stage, c, there],
                dev(pipe, ctx, there),
            ).wait()
        value = st_recv[stage, c, 0]
        for d in range(1, ndp):
            value = value + st_recv[stage, c, d]
        value = fn(value)
        base = first_octet(many, c)
        for k in range(span(many)):
            put_rows(stage + 1, base + k, value, base + k)

    def collect(many, c):
        base = first_octet(many, c)
        value = zero
        for n in range(span(many)):
            acc = None
            for k in range(SUB):
                piece = parts[pl.ds((base + n) * SUB * SUB + k, SUB, stride=SUB), :]
                acc = piece if acc is None else acc + piece
            value = jnp.where(lane == base + n, jnp.sum(acc, axis=1, keepdims=True), value)
        return value

    per = groups // teams

    def spot(k, g):
        return pl.ds(k * nb + g * SUB if isinstance(g, int) else pl.multiple_of(k * nb + g * SUB, SUB), SUB)

    def build_filters(b, team):
        for n in range(per):
            g = team * per + n
            first = n * SUB // cb
            many = max(SUB // cb, 1)
            for k in range(ntap):
                if cb >= SUB:
                    z, row = n * SUB // cb, n * SUB % cb
                    value = fr[b, team * slabs + z, k * cb + row : k * cb + row + SUB, :]
                else:
                    value = jnp.concatenate(
                        [fr[b, team * slabs + first + s, k * cb : (k + 1) * cb, :] for s in range(many)], axis=0
                    )
                filt[b, spot(k, g), :] = value
                if k == 0:
                    gain = value
                elif k <= nshort:
                    fold[b, spot(k - 1, g), :] = value * gain

    def at(w, g):
        return pl.ds(pl.multiple_of((g * total + w) * SUB, SUB), SUB)

    def row_of(stage, w):
        return jnp.broadcast_to(rows[stage, pl.ds(w, 1), :], (SUB, LANES))

    def kept(ref, b, g, count, i):
        return ref.at[pl.ds(((b * groups + g) * count + i) * SUB, SUB), :]

    def add_part(w, g, value):
        here = at(w, 0)
        parts[here, :] = value if g == 0 else parts[here, :] + value

    def forward(b, c, start, unroll):
        part, chunks = nrow // ahead, ahead
        lo = jnp.where(c == 0, start, halo + part * c)
        hi = jnp.where(c == chunks - 1, total, halo + part * (c + 1))

        def step(it, _):
            for g in range(groups):
                short = [fold[b, spot(k, g), :] for k in range(nshort)]
                long = [filt[b, spot(1 + nshort + k, g), :] for k in range(nlong)]
                held = [kept(fstate, b, g, nfwd, i) for i in range(nfwd)]
                lag = [ref[...] for ref in held[: taps - 1]]
                past = [ref[...] for ref in held[taps - 1 :]]
                for u in range(unroll):
                    w = lo + it * unroll + u
                    x = (xs if b == 0 else ys)[at(w, g), :]
                    xh = x * row_of(b, w)
                    seq = [xh] + lag
                    streams = []
                    for j in range(3):
                        value = short[taps * j] * seq[0]
                        for i in range(1, taps):
                            value = value + short[taps * j + i] * seq[i]
                        streams.append(value)
                    products = [streams[1] * streams[2]] + past
                    mix = long[0] * products[0]
                    for i in range(1, nlong):
                        mix = mix + long[i] * products[i]
                    for n, value in enumerate((xh, streams[0], streams[1], streams[2], mix, products[0])):
                        saved[b, n, at(w, g), :] = value
                    if b == 0:
                        inner = (x + streams[0] * mix).astype(BF16).astype(F32)
                        ys[at(w, g), :] = inner
                        add_part(w, g, inner * inner)
                    lag, past = seq[:-1], products[:-1]
                for ref, value in zip(held, lag + past):
                    ref[...] = value
            return 0

        lax.fori_loop(0, (hi - lo) // unroll, step, 0)

    for o in range(1, nctx):
        wait_filters(0, o)
    for n in range(teams):
        build_filters(0, n)

    def ahead_inner(c, _):
        forward(0, c, 0, ahead_rows)
        send_stat(0, c, collect(ahead, c))
        return 0

    lax.fori_loop(0, ahead, ahead_inner, 0)

    for o in range(1, nctx):
        wait_filters(1, o)
    for n in range(teams):
        build_filters(1, n)

    def ahead_outer(c, _):
        get_stat(0, ahead, c, row_scale)
        forward(1, c, 0, ahead_rows)
        return 0

    lax.fori_loop(0, ahead, ahead_outer, 0)

    @pl.when(has_down)
    def _():
        remote(cbot, cbot, halo_send.at[2], halo_recv.at[2], dev(follow, down_z, dp)).wait_recv()

    @pl.when(jnp.logical_not(has_down))
    def _():
        cbot[...] = jnp.zeros(cbot.shape, BF16)

    spread(zs, halo + nrow, cbot[...].astype(F32))

    def take_cot(i, _):
        spread(zs, halo + i * 16, cbuf[pl.ds(pl.multiple_of(i * 16, 16), 16), :].astype(F32))
        return 0

    def backward(b, c, top, brief, unroll):
        lo = halo + part * c
        hi = lo + part

        def one(g, w, short, long, state, acc):
            dmix_next, ds_next = state
            here = at(w, g)
            up = zs[here, :]
            if b == 0:
                up = up + row_of(1, w) * (wd_outer[here, :] - saved[1, 0, here, :] * row_of(2, w))
                xs[here, :] = up
            xh, query, key, value, mix, product = [saved[b, n, here, :] for n in range(6)]
            dmix = [up * query] + dmix_next
            dprod = long[0] * dmix[0]
            for i in range(1, nlong):
                dprod = dprod + long[i] * dmix[i]
            ds = [[up * mix] + ds_next[0], [dprod * value] + ds_next[1], [dprod * key] + ds_next[2]]
            weighted = None
            for j in range(3):
                for i in range(taps):
                    term = short[taps * j + i] * ds[j][i]
                    weighted = term if weighted is None else weighted + term
            (wd_outer if b == 1 else wd_inner)[here, :] = weighted
            add_part(w, g, xh * weighted)
            if acc is not None:
                fresh = []
                for j in range(3):
                    for i in range(taps):
                        fresh.append(acc[taps * j + i] + xh * ds[j][i])
                for i in range(nlong):
                    fresh.append(acc[nshort + i] + product * dmix[i])
                acc = fresh
            return (dmix[:-1], [d[:-1] for d in ds]), acc

        def flat(state):
            return list(state[0]) + [v for d in state[1] for v in d]

        def unflat(vals):
            n = nlong - 1
            rest = vals[n:]
            m = taps - 1
            return list(vals[:n]), [list(rest[j * m : (j + 1) * m]) for j in range(3)]

        def rows_back(high, many, summed):
            def step(it, _):
                for g in range(groups):
                    short = [fold[b, spot(k, g), :] for k in range(nshort)]
                    long = [filt[b, spot(1 + nshort + k, g), :] for k in range(nlong)]
                    held = [kept(bstate, b, g, nbwd, i) for i in range(nbwd)]
                    state = unflat([ref[...] for ref in held])
                    acc = [grads[b, spot(k, g), :] for k in range(1, ntap)] if summed else None
                    for u in range(many):
                        state, acc = one(g, high - 1 - it * many - u, short, long, state, acc)
                    for ref, value in zip(held, flat(state)):
                        ref[...] = value
                    if summed:
                        for k in range(1, ntap):
                            grads[b, spot(k, g), :] = acc[k - 1]
                return 0

            return step

        extra = jnp.where(c == chunks - 1, (top - halo - nrow) // brief, 0)
        lax.fori_loop(0, extra, rows_back(top, brief, False), 0)
        lax.fori_loop(0, part // unroll, rows_back(hi, unroll, True), 0)

    def back_outer(it, _):
        c = chunks - 1 - it
        remote(
            cbuf.at[rows_of(c), :], cbuf.at[rows_of(c), :], c_send.at[c], c_recv.at[c], dev(follow, ctx, dp)
        ).wait_recv()
        lax.fori_loop(c * (part // 16), (c + 1) * (part // 16), take_cot, 0)
        backward(1, c, total, 8, back_rows)
        send_stat(1, c, collect(chunks, c))
        return 0

    lax.fori_loop(0, chunks, back_outer, 0)

    def finish_grads(b):
        for g in range(groups):
            gain = filt[b, spot(0, g), :]
            acc = None
            for k in range(1, 1 + nshort):
                raw = grads[b, spot(k, g), :]
                term = raw * filt[b, spot(k, g), :]
                acc = term if acc is None else acc + term
                grads[b, spot(k, g), :] = raw * gain
            grads[b, spot(0, g), :] = acc

    finish_grads(1)
    to_follow = remote(grads.at[1], gin, p_send.at[0], p_recv.at[0], dev(follow, ctx, dp))
    to_follow.start()

    def send_grads(o):
        z = ctx_at(o)
        return remote(gsent.at[z], rg.at[ctx], g_send.at[o], g_recv.at[ctx], dev(pipe, z, dp))

    def share_grads():
        finish_grads(0)
        remote(grads.at[1], gin, p_send.at[0], p_recv.at[0], dev(prev, ctx, dp)).wait_recv()
        for z in range(nctx):
            for k in range(ntap):
                here = pl.ds(k * nb + z * cb, cb)
                gs[z, k * cb : (k + 1) * cb, :] = grads[0, here, :] + gin[here, :]
            gsent[z] = gs[z].astype(BF16)
        for o in range(1, nctx):
            send_grads(o).start()

    def back_inner(it, _):
        c = chunks - 1 - it
        get_stat(1, chunks, c, mean_of)
        backward(0, c, halo + nrow + halo // 2, 8, back_rows)

        @pl.when(c == 0)
        def _():
            share_grads()

        send_stat(2, c, collect(chunks, c))
        return 0

    lax.fori_loop(0, chunks, back_inner, 0)

    def finish(i, _):
        w = halo + i * 16
        halves = [pl.multiple_of(w + half * SUB, SUB) for half in range(2)]
        scales = [rows[0, pl.ds(h, SUB), :] for h in halves]
        means = [rows[3, pl.ds(h, SUB), :] for h in halves]
        for j in range(nb):
            pieces = []
            for half in range(2):
                here = pl.ds(j // SUB * total * SUB + halves[half] * SUB + j % SUB, SUB, stride=SUB)
                pieces.append(xs[here, :] + scales[half] * (wd_inner[here, :] - saved[0, 0, here, :] * means[half]))
            out[0, pl.ds(pl.multiple_of(i * 16, 16), 16), j * LANES : (j + 1) * LANES] = jnp.concatenate(
                pieces, axis=0
            ).astype(BF16)
        return 0

    def wind_up(it, _):
        c = chunks - 1 - it
        get_stat(2, chunks, c, mean_of)
        lax.fori_loop(c * (part // 16), (c + 1) * (part // 16), finish, 0)
        return 0

    lax.fori_loop(0, chunks, wind_up, 0)

    for c in range(chunks):
        to_cot(c).wait_send()

    @pl.when(has_up)
    def _():
        to_bot.wait_send()
        to_cbot.wait_send()
        for o in range(ndp):
            to_stat0(2, o, up_z).wait_send()

    @pl.when(has_down)
    def _():
        to_top.wait_send()
        for o in range(ndp):
            to_stat0(0, o, down_z).wait_send()

    for o in range(1, ndp):
        to_stat0(1, o, ctx).wait_send()
    for o in range(1, nctx):
        send_filters(0, o).wait_send()
        send_filters(1, o).wait_send()
    to_prev.wait_send()
    to_follow.wait_send()

    for o in range(1, nctx):
        z = ctx_at(o)
        remote(gsent.at[z], rg.at[z], g_send.at[o], g_recv.at[z], dev(pipe, z, dp)).wait_recv()
    result = gs[ctx]
    for o in range(1, nctx):
        result = result + rg[ctx_at(o)].astype(F32)
    for k in range(ntap):
        for j in range(cb):
            cols = pl.ds(j * LANES, LANES)
            piece = result[k * cb + j : k * cb + j + 1, :]
            if k == 0:
                gain_out[0:1, cols] = piece
            elif k <= nshort:
                short_out[k - 1, 0:1, cols] = piece
            else:
                long_out[k - 1 - nshort, 0:1, cols] = piece

    for o in range(1, nctx):
        send_grads(o).wait_send()


def handed_on(a0, a1, a2, a3, b0, b1, b2, b3, sem):
    half = a0.shape[1] // 2
    pairs = [(a0.at[0, pl.ds(i * half, half), :], b0.at[0, pl.ds(i * half, half), :]) for i in range(2)]
    copies = [
        pltpu.make_async_copy(a, b, sem.at[i]) for i, (a, b) in enumerate(pairs + [(a1, b1), (a2, b2), (a3, b3)])
    ]
    for c in copies:
        c.start()
    for c in copies:
        c.wait()


def swap(values):
    return jnp.transpose(values, (1, 0, 2))


def per_device(mesh, hidden, cotangent, gain_rows, short_taps, long_taps):
    npipe, nctx, ndp = mesh.shape["pipe"], mesh.shape["ctx"], mesh.shape["dp"]
    nrow, chans = hidden.shape[1], hidden.shape[2]
    own = gain_rows.shape[1]
    wide = -(-own // LANES) * LANES
    nshort, nlong = short_taps.shape[1], long_taps.shape[1]
    ntap = 1 + nshort + nlong
    cb = wide // LANES
    nb = nctx * cb
    halo = 2 * (nshort // 3 + nlong - 2)
    total = nrow + 2 * halo
    slab_rows = -(-ntap * cb // 16) * 16
    ahead = next(n for n in (2, 1) if nrow % (16 * n) == 0)
    chunks = next(n for n in (BACK, 1) if nrow % (16 * n) == 0)
    groups = nb // SUB
    nfwd = nshort // 3 - 1 + nlong - 1
    nbwd = nlong - 1 + 3 * (nshort // 3 - 1)

    def widen(values):
        if wide == own:
            return values
        lead = values.shape[:-1]
        blocks = values.reshape(lead + (-1, own))
        blocks = jnp.pad(blocks, [(0, 0)] * (len(lead) + 1) + [(0, wide - own)])
        return blocks.reshape(lead + (-1,))

    def narrow(values):
        if wide == own:
            return values
        lead = values.shape[:-1]
        return values.reshape(lead + (-1, wide))[..., :own].reshape(lead + (-1,))

    cfg = dict(
        npipe=npipe, nctx=nctx, ndp=ndp, nrow=nrow, nb=nb, cb=cb, ntap=ntap, nshort=nshort,
        width=float(chans * ndp), halo=halo, ahead=ahead, chunks=chunks,
    )
    full = nb * LANES
    dma = pltpu.SemaphoreType.DMA
    vmem = pl.BlockSpec(memory_space=pltpu.VMEM)
    anywhere = pl.BlockSpec(memory_space=pl.ANY)
    shapes = (
        jax.ShapeDtypeStruct((1, nrow, full), BF16),
        jax.ShapeDtypeStruct((1, wide), F32),
        jax.ShapeDtypeStruct((nshort, 1, wide), F32),
        jax.ShapeDtypeStruct((nlong, 1, wide), F32),
    )
    outs = pl.pallas_call(
        functools.partial(kernel, cfg),
        out_shape=tuple(pltpu.VMEM(s.shape, s.dtype) for s in shapes),
        in_specs=[anywhere] * 5,
        out_specs=(vmem,) * 4,
        scratch_shapes=[
            pltpu.VMEM((1, wide), F32),
            pltpu.VMEM((nshort, 1, wide), F32),
            pltpu.VMEM((nlong, 1, wide), F32),
            pltpu.VMEM((nrow, full), BF16),
            pltpu.VMEM((halo, full), BF16),
            pltpu.VMEM((halo, full), BF16),
            pltpu.VMEM((nrow, full), BF16),
            pltpu.VMEM((halo, full), BF16),
            pltpu.VMEM((slab_rows, LANES), F32),
            pltpu.VMEM((2, nctx, slab_rows, LANES), F32),
            pltpu.VMEM((2, ntap * nb, LANES), F32),
            pltpu.VMEM((2, nshort * nb, LANES), F32),
            pltpu.VMEM((2, ntap * nb, LANES), F32),
            pltpu.VMEM((ntap * nb, LANES), F32),
            pltpu.VMEM((nctx, slab_rows, LANES), F32),
            pltpu.VMEM((nctx, slab_rows, LANES), BF16),
            pltpu.VMEM((nctx, slab_rows, LANES), BF16),
            pltpu.VMEM((total * nb, LANES), F32),
            pltpu.VMEM((total * nb, LANES), F32),
            pltpu.VMEM((total * nb, LANES), F32),
            pltpu.VMEM((total * nb, LANES), F32),
            pltpu.VMEM((total * nb, LANES), F32),
            pltpu.VMEM((2, 6, total * nb, LANES), F32),
            pltpu.VMEM((total * SUB, LANES), F32),
            pltpu.VMEM((2 * groups * nfwd * SUB, LANES), F32),
            pltpu.VMEM((2 * groups * nbwd * SUB, LANES), F32),
            pltpu.VMEM((SUB, LANES), F32),
            pltpu.VMEM((3, ndp, SUB, LANES), F32),
            pltpu.VMEM((3, ahead, SUB, LANES), F32),
            pltpu.VMEM((3, ahead, ndp, SUB, LANES), F32),
            pltpu.VMEM((4, total, LANES), F32),
            dma((chunks,)),
            dma((3,)),
            dma((3,)),
            dma((3,)),
            dma((chunks,)),
            dma((chunks,)),
            dma((2, nctx)),
            dma((2, nctx)),
            dma((1,)),
            dma((1,)),
            dma((nctx,)),
            dma((nctx,)),
            dma((3, ndp)),
            dma((3, ndp)),
            dma((3, ahead, ndp)),
            dma((3, ahead, ndp)),
        ],
        compiler_params=pltpu.CompilerParams(
            collective_id=0, has_side_effects=True, vmem_limit_bytes=62 * 1024 * 1024 - 1400 * 1024
        ),
        name="relay",
    )(widen(hidden), widen(cotangent), widen(gain_rows), swap(widen(short_taps)), swap(widen(long_taps)))
    outs = pl.pallas_call(
        handed_on,
        out_shape=shapes,
        in_specs=[vmem] * 4,
        out_specs=(anywhere,) * 4,
        scratch_shapes=[dma((5,))],
        compiler_params=pltpu.CompilerParams(vmem_limit_bytes=4 * 1024 * 1024),
        name="handed_on",
    )(*outs)
    return tuple(narrow(o) for o in (outs[0], outs[1], swap(outs[2]), swap(outs[3])))


def solution(mesh):
    in_specs = (
        P("pipe", "ctx", "dp"),
        P("pipe", "ctx", "dp"),
        P("pipe", ("dp", "ctx")),
        P("pipe", None, ("dp", "ctx")),
        P("pipe", None, ("dp", "ctx")),
    )
    out_specs = (
        P("pipe", "ctx", "dp"),
        P("pipe", ("dp", "ctx")),
        P("pipe", None, ("dp", "ctx")),
        P("pipe", None, ("dp", "ctx")),
    )
    return jax.shard_map(
        functools.partial(per_device, mesh), mesh=mesh, in_specs=in_specs, out_specs=out_specs, check_vma=False
    )
```

```python
import functools

import jax
import jax.numpy as jnp
from jax import lax
from jax.experimental import pallas as pl
from jax.experimental.pallas import tpu as pltpu
from jax.sharding import PartitionSpec as P

MESH = pl.DeviceIdType.MESH
F32 = jnp.float32
BF16 = jnp.bfloat16
LANES = 128
SUB = 8
EPS = 1e-05
BACK = 2


def kernel(
    cfg,
    hid,
    cot,
    gain_hbm,
    short_hbm,
    long_hbm,
    out,
    gain_out,
    short_out,
    long_out,
    gain_in,
    short_in,
    long_in,
    hbuf,
    htop,
    hbot,
    cbuf,
    cbot,
    slab,
    fr,
    filt,
    fold,
    grads,
    gin,
    gs,
    gsent,
    rg,
    xs,
    ys,
    zs,
    wd_outer,
    wd_inner,
    saved,
    parts,
    fstate,
    bstate,
    st0_send,
    st0_recv,
    st_send,
    st_recv,
    rows,
    in_sem,
    small_sem,
    halo_send,
    halo_recv,
    c_send,
    c_recv,
    f_send,
    f_recv,
    p_send,
    p_recv,
    g_send,
    g_recv,
    s0_send,
    s0_recv,
    s_send,
    s_recv,
):
    npipe, nctx, ndp = cfg["npipe"], cfg["nctx"], cfg["ndp"]
    nrow, nb, cb, ntap, nshort, width = (
        cfg["nrow"], cfg["nb"], cfg["cb"], cfg["ntap"], cfg["nshort"], cfg["width"],
    )
    ahead, chunks = cfg["ahead"], cfg["chunks"]
    taps = nshort // 3
    nlong = ntap - 1 - nshort
    halo = cfg["halo"]
    total = nrow + 2 * halo
    part = nrow // chunks
    reach = nrow // ahead + (halo if ahead == 2 else 2 * halo)
    ahead_rows = next(n for n in (24, 16, 8) if reach % n == 0)
    back_rows = next(n for n in (32, 16) if part % n == 0)
    groups = nb // SUB
    edge = halo // SUB
    slabs = SUB // cb if cb < SUB and SUB % cb == 0 else nctx
    slabs = min(slabs, nctx)
    teams = nctx // slabs
    nfwd = taps - 1 + nlong - 1
    nbwd = nlong - 1 + 3 * (taps - 1)
    pipe, ctx, dp = lax.axis_index("pipe"), lax.axis_index("ctx"), lax.axis_index("dp")
    prev = lax.rem(pipe + npipe - 1, npipe)
    follow = lax.rem(pipe + 1, npipe)

    def ctx_at(o):
        return lax.rem(ctx + o, nctx)

    def dp_at(o):
        return lax.rem(dp + o, ndp)

    def team_at(o):
        team = lax.rem(ctx // slabs + o // slabs, teams)
        return team * slabs + lax.rem(lax.rem(ctx, slabs) + o % slabs, slabs)

    def dev(p, z, d):
        return {"pipe": p, "ctx": z, "dp": d}

    def remote(src, dst, ss, rs, where):
        return pltpu.make_async_remote_copy(
            src_ref=src, dst_ref=dst, send_sem=ss, recv_sem=rs, device_id=where, device_id_type=MESH
        )

    barrier = pltpu.get_barrier_semaphore()
    peers = [(pipe, ctx_at(o), dp) for o in range(1, nctx)]
    for d in range(1, ndp):
        for o in sorted({0, 1 % nctx, (nctx - 1) % nctx}):
            peers.append((pipe, ctx_at(o), dp_at(d)))
    peers += [(prev, ctx, dp), (follow, ctx, dp), (follow, ctx_at(1), dp)]
    for p, z, d in peers:
        pl.semaphore_signal(barrier, inc=1, device_id=dev(p, z, d), device_id_type=MESH)

    def rows_of(c):
        return pl.ds(c * part, part)

    def load_hid(c):
        return pltpu.make_async_copy(hid.at[0, rows_of(c), :], hbuf.at[rows_of(c), :], in_sem.at[c])

    small = [
        pltpu.make_async_copy(a, b, small_sem.at[i])
        for i, (a, b) in enumerate(((gain_hbm, gain_in), (short_hbm, short_in), (long_hbm, long_in)))
    ]
    for copy in small:
        copy.start()
    for c in range(chunks):
        load_hid(c).start()

    zero = jnp.zeros((SUB, LANES), F32)
    for i in range(2 * groups * nfwd):
        fstate[i * SUB : (i + 1) * SUB, :] = zero
    for i in range(2 * groups * nbwd):
        bstate[i * SUB : (i + 1) * SUB, :] = zero
    for i in range(2 * ntap * groups):
        grads[i // (ntap * groups), i % (ntap * groups) * SUB : (i % (ntap * groups) + 1) * SUB, :] = zero

    lane = lax.broadcasted_iota(jnp.int32, (SUB, LANES), 1)

    def spread(dst, first, block):
        for half in range(2):
            piece = block[half * SUB : (half + 1) * SUB, :]
            start = (first + half * SUB) * SUB
            for j in range(nb):
                dst[pl.ds(j // SUB * total * SUB + start + j % SUB, SUB, stride=SUB), :] = piece[:, j * LANES : (j + 1) * LANES]

    def squares(stat, first, block):
        for half in range(2):
            acc = None
            for j in range(nb):
                piece = block[half * SUB : (half + 1) * SUB, j * LANES : (j + 1) * LANES]
                acc = piece * piece if acc is None else acc + piece * piece
            value = jnp.sum(acc, axis=1, keepdims=True)
            stat = jnp.where(lane == first // SUB + half, value, stat)
        return stat

    def take_hidden(i, stat):
        block = hbuf[pl.ds(pl.multiple_of(i * 16, 16), 16), :].astype(F32)
        spread(xs, halo + i * 16, block)
        return squares(stat, halo + i * 16, block)

    for copy in small:
        copy.wait()
    for k in range(ntap):
        src, row = (gain_in, 0) if k == 0 else ((short_in, k - 1) if k <= nshort else (long_in, k - 1 - nshort))
        for j in range(cb):
            cols = pl.ds(j * LANES, LANES)
            piece = src[row : row + 1, cols] if k == 0 else src[row, 0:1, cols]
            slab[k * cb + j : k * cb + j + 1, :] = piece
    pad = slab.shape[0] - ntap * cb
    if pad:
        slab[ntap * cb :, :] = jnp.zeros((pad, LANES), F32)
        for z in range(nctx):
            gs[z, ntap * cb :, :] = jnp.zeros((pad, LANES), F32)
    fr[0, ctx] = slab[...]
    stat = zero
    for c in range(chunks):
        load_hid(c).wait()
        stat = lax.fori_loop(c * part // 16, (c + 1) * part // 16, take_hidden, stat)
    st0_send[...] = stat
    st0_recv[1, dp] = stat

    pl.semaphore_wait(barrier, len(peers))

    up_z = lax.max(ctx - 1, 0)
    down_z = lax.min(ctx + 1, nctx - 1)
    head, tail = pl.ds(0, halo), pl.ds(nrow - halo, halo)
    to_bot = remote(hbuf.at[head, :], hbot, halo_send.at[0], halo_recv.at[0], dev(pipe, up_z, dp))
    to_top = remote(hbuf.at[tail, :], htop, halo_send.at[1], halo_recv.at[1], dev(pipe, down_z, dp))
    to_cbot = remote(cot.at[0, head, :], cbot, halo_send.at[2], halo_recv.at[2], dev(prev, up_z, dp))
    has_up, has_down = ctx > 0, ctx < nctx - 1

    def send_filters(b, o):
        mine = fr.at[1, ctx] if b else slab
        return remote(mine, fr.at[b, ctx], f_send.at[b, o], f_recv.at[b, ctx], dev(pipe, team_at(o), dp))

    def wait_filters(b, o):
        there = team_at(o)
        remote(slab, fr.at[b, there], f_send.at[b, o], f_recv.at[b, there], dev(pipe, there, dp)).wait_recv()

    to_prev = remote(slab, fr.at[1, ctx], f_send.at[1, 0], f_recv.at[1, ctx], dev(prev, ctx, dp))

    def to_stat0(slot, o, z):
        return remote(st0_send, st0_recv.at[slot, dp], s0_send.at[slot, o], s0_recv.at[slot, dp], dev(pipe, z, dp_at(o)))

    def from_stat0(slot, o, z):
        there = dp_at(o)
        return remote(
            st0_send, st0_recv.at[slot, there], s0_send.at[slot, o], s0_recv.at[slot, there], dev(pipe, z, there)
        )

    for o in range(1, ndp):
        to_stat0(1, o, ctx).start()

    @pl.when(has_down)
    def _():
        for o in range(ndp):
            to_stat0(0, o, down_z).start()

    @pl.when(has_up)
    def _():
        for o in range(ndp):
            to_stat0(2, o, up_z).start()

    for o in range(nctx - 1, 1, -1):
        send_filters(0, o).start()

    @pl.when(has_down)
    def _():
        to_top.start()

    send_filters(0, 1).start()

    @pl.when(has_up)
    def _():
        to_bot.start()
        to_cbot.start()

    def to_cot(c):
        return remote(
            cot.at[0, rows_of(c), :], cbuf.at[rows_of(c), :], c_send.at[c], c_recv.at[c], dev(prev, ctx, dp)
        )

    to_prev.start()
    for c in range(chunks - 1, -1, -1):
        to_cot(c).start()

    @pl.when(has_up)
    def _():
        remote(htop, htop, halo_send.at[1], halo_recv.at[1], dev(pipe, up_z, dp)).wait_recv()
        for o in range(ndp):
            from_stat0(0, o, up_z).wait_recv()

    @pl.when(jnp.logical_not(has_up))
    def _():
        htop[...] = jnp.zeros(htop.shape, BF16)
        for d in range(ndp):
            st0_recv[0, d] = zero

    @pl.when(has_down)
    def _():
        remote(hbot, hbot, halo_send.at[0], halo_recv.at[0], dev(pipe, down_z, dp)).wait_recv()
        for o in range(ndp):
            from_stat0(2, o, down_z).wait_recv()

    @pl.when(jnp.logical_not(has_down))
    def _():
        hbot[...] = jnp.zeros(hbot.shape, BF16)
        for d in range(ndp):
            st0_recv[2, d] = zero

    remote(slab, fr.at[1, ctx], f_send.at[1, 0], f_recv.at[1, ctx], dev(follow, ctx, dp)).wait_recv()
    for o in range(1, nctx):
        send_filters(1, o).start()

    spread(xs, 0, htop[...].astype(F32))
    spread(xs, halo + nrow, hbot[...].astype(F32))

    def row_scale(value):
        return lax.rsqrt(value / width + EPS)

    def mean_of(value):
        return value / width

    def put_rows(stage, at_octet, value, i):
        column = jnp.sum(jnp.where(lane == i, value, 0.0), axis=1, keepdims=True)
        rows[stage, pl.ds(pl.multiple_of(at_octet * SUB, SUB), SUB), :] = jnp.broadcast_to(column, (SUB, LANES))

    for o in range(1, ndp):
        from_stat0(1, o, ctx).wait_recv()
    sums = []
    for slot in range(3):
        value = st0_recv[slot, 0]
        for d in range(1, ndp):
            value = value + st0_recv[slot, d]
        sums.append(row_scale(value))
    for i in range(edge):
        put_rows(0, i, sums[0], i + nrow // SUB)
        put_rows(0, edge + nrow // SUB + i, sums[2], i + edge)
    for i in range(edge, edge + nrow // SUB):
        put_rows(0, i, sums[1], i)

    def first_octet(many, c):
        return jnp.where(c == 0, 0, edge + nrow // SUB // many * c)

    def span(many):
        return nrow // SUB // many + edge

    def send_stat(stage, c, value):
        st_send[stage, c] = value
        st_recv[stage, c, dp] = value
        for o in range(1, ndp):
            remote(
                st_send.at[stage, c], st_recv.at[stage, c, dp], s_send.at[stage, c, o], s_recv.at[stage, c, dp],
                dev(pipe, ctx, dp_at(o)),
            ).start()

    def get_stat(stage, many, c, fn):
        for o in range(1, ndp):
            there = dp_at(o)
            remote(
                st_send.at[stage, c], st_recv.at[stage, c, there], s_send.at[stage, c, o], s_recv.at[stage, c, there],
                dev(pipe, ctx, there),
            ).wait()
        value = st_recv[stage, c, 0]
        for d in range(1, ndp):
            value = value + st_recv[stage, c, d]
        value = fn(value)
        base = first_octet(many, c)
        for k in range(span(many)):
            put_rows(stage + 1, base + k, value, base + k)

    def collect(many, c):
        base = first_octet(many, c)
        value = zero
        for n in range(span(many)):
            acc = None
            for k in range(SUB):
                piece = parts[pl.ds((base + n) * SUB * SUB + k, SUB, stride=SUB), :]
                acc = piece if acc is None else acc + piece
            value = jnp.where(lane == base + n, jnp.sum(acc, axis=1, keepdims=True), value)
        return value

    per = groups // teams

    def spot(k, g):
        return pl.ds(k * nb + g * SUB if isinstance(g, int) else pl.multiple_of(k * nb + g * SUB, SUB), SUB)

    def build_filters(b, team):
        for n in range(per):
            g = team * per + n
            first = n * SUB // cb
            many = max(SUB // cb, 1)
            for k in range(ntap):
                if cb >= SUB:
                    z, row = n * SUB // cb, n * SUB % cb
                    value = fr[b, team * slabs + z, k * cb + row : k * cb + row + SUB, :]
                else:
                    value = jnp.concatenate(
                        [fr[b, team * slabs + first + s, k * cb : (k + 1) * cb, :] for s in range(many)], axis=0
                    )
                filt[b, spot(k, g), :] = value
                if k == 0:
                    gain = value
                elif k <= nshort:
                    fold[b, spot(k - 1, g), :] = value * gain

    def at(w, g):
        return pl.ds(pl.multiple_of((g * total + w) * SUB, SUB), SUB)

    def row_of(stage, w):
        return jnp.broadcast_to(rows[stage, pl.ds(w, 1), :], (SUB, LANES))

    def kept(ref, b, g, count, i):
        return ref.at[pl.ds(((b * groups + g) * count + i) * SUB, SUB), :]

    def add_part(w, g, value):
        here = at(w, 0)
        parts[here, :] = value if g == 0 else parts[here, :] + value

    def forward(b, c, start, unroll):
        part, chunks = nrow // ahead, ahead
        lo = jnp.where(c == 0, start, halo + part * c)
        hi = jnp.where(c == chunks - 1, total, halo + part * (c + 1))

        def step(it, _):
            for g in range(groups):
                short = [fold[b, spot(k, g), :] for k in range(nshort)]
                long = [filt[b, spot(1 + nshort + k, g), :] for k in range(nlong)]
                held = [kept(fstate, b, g, nfwd, i) for i in range(nfwd)]
                lag = [ref[...] for ref in held[: taps - 1]]
                past = [ref[...] for ref in held[taps - 1 :]]
                for u in range(unroll):
                    w = lo + it * unroll + u
                    x = (xs if b == 0 else ys)[at(w, g), :]
                    xh = x * row_of(b, w)
                    seq = [xh] + lag
                    streams = []
                    for j in range(3):
                        value = short[taps * j] * seq[0]
                        for i in range(1, taps):
                            value = value + short[taps * j + i] * seq[i]
                        streams.append(value)
                    products = [streams[1] * streams[2]] + past
                    mix = long[0] * products[0]
                    for i in range(1, nlong):
                        mix = mix + long[i] * products[i]
                    for n, value in enumerate((xh, streams[0], streams[1], streams[2], mix, products[0])):
                        saved[b, n, at(w, g), :] = value
                    if b == 0:
                        inner = (x + streams[0] * mix).astype(BF16).astype(F32)
                        ys[at(w, g), :] = inner
                        add_part(w, g, inner * inner)
                    lag, past = seq[:-1], products[:-1]
                for ref, value in zip(held, lag + past):
                    ref[...] = value
            return 0

        lax.fori_loop(0, (hi - lo) // unroll, step, 0)

    for o in range(1, nctx):
        wait_filters(0, o)
    for n in range(teams):
        build_filters(0, n)

    def ahead_inner(c, _):
        forward(0, c, 0, ahead_rows)
        send_stat(0, c, collect(ahead, c))
        return 0

    lax.fori_loop(0, ahead, ahead_inner, 0)

    for o in range(1, nctx):
        wait_filters(1, o)
    for n in range(teams):
        build_filters(1, n)

    def ahead_outer(c, _):
        get_stat(0, ahead, c, row_scale)
        forward(1, c, 0, ahead_rows)
        return 0

    lax.fori_loop(0, ahead, ahead_outer, 0)

    @pl.when(has_down)
    def _():
        remote(cbot, cbot, halo_send.at[2], halo_recv.at[2], dev(follow, down_z, dp)).wait_recv()

    @pl.when(jnp.logical_not(has_down))
    def _():
        cbot[...] = jnp.zeros(cbot.shape, BF16)

    spread(zs, halo + nrow, cbot[...].astype(F32))

    def take_cot(n, _):
        for i in (2 * n, 2 * n + 1):
            spread(zs, halo + i * 16, cbuf[pl.ds(pl.multiple_of(i * 16, 16), 16), :].astype(F32))
        return 0

    def backward(b, c, top, brief, unroll):
        lo = halo + part * c
        hi = lo + part

        def one(g, w, short, long, state, acc):
            dmix_next, ds_next = state
            here = at(w, g)
            up = zs[here, :]
            if b == 0:
                up = up + row_of(1, w) * (wd_outer[here, :] - saved[1, 0, here, :] * row_of(2, w))
                xs[here, :] = up
            xh, query, key, value, mix, product = [saved[b, n, here, :] for n in range(6)]
            dmix = [up * query] + dmix_next
            dprod = long[0] * dmix[0]
            for i in range(1, nlong):
                dprod = dprod + long[i] * dmix[i]
            ds = [[up * mix] + ds_next[0], [dprod * value] + ds_next[1], [dprod * key] + ds_next[2]]
            weighted = None
            for j in range(3):
                for i in range(taps):
                    term = short[taps * j + i] * ds[j][i]
                    weighted = term if weighted is None else weighted + term
            (wd_outer if b == 1 else wd_inner)[here, :] = weighted
            add_part(w, g, xh * weighted)
            if acc is not None:
                fresh = []
                for j in range(3):
                    for i in range(taps):
                        fresh.append(acc[taps * j + i] + xh * ds[j][i])
                for i in range(nlong):
                    fresh.append(acc[nshort + i] + product * dmix[i])
                acc = fresh
            return (dmix[:-1], [d[:-1] for d in ds]), acc

        def flat(state):
            return list(state[0]) + [v for d in state[1] for v in d]

        def unflat(vals):
            n = nlong - 1
            rest = vals[n:]
            m = taps - 1
            return list(vals[:n]), [list(rest[j * m : (j + 1) * m]) for j in range(3)]

        def rows_back(high, many, summed):
            def step(it, _):
                for g in range(groups):
                    short = [fold[b, spot(k, g), :] for k in range(nshort)]
                    long = [filt[b, spot(1 + nshort + k, g), :] for k in range(nlong)]
                    held = [kept(bstate, b, g, nbwd, i) for i in range(nbwd)]
                    state = unflat([ref[...] for ref in held])
                    acc = [grads[b, spot(k, g), :] for k in range(1, ntap)] if summed else None
                    for u in range(many):
                        state, acc = one(g, high - 1 - it * many - u, short, long, state, acc)
                    for ref, value in zip(held, flat(state)):
                        ref[...] = value
                    if summed:
                        for k in range(1, ntap):
                            grads[b, spot(k, g), :] = acc[k - 1]
                return 0

            return step

        extra = jnp.where(c == chunks - 1, (top - halo - nrow) // brief, 0)
        lax.fori_loop(0, extra, rows_back(top, brief, False), 0)
        lax.fori_loop(0, part // unroll, rows_back(hi, unroll, True), 0)

    def back_outer(it, _):
        c = chunks - 1 - it
        remote(
            cbuf.at[rows_of(c), :], cbuf.at[rows_of(c), :], c_send.at[c], c_recv.at[c], dev(follow, ctx, dp)
        ).wait_recv()
        lax.fori_loop(c * (part // 32), (c + 1) * (part // 32), take_cot, 0)
        backward(1, c, total, 8, back_rows)
        send_stat(1, c, collect(chunks, c))
        return 0

    lax.fori_loop(0, chunks, back_outer, 0)

    def finish_grads(b):
        for g in range(groups):
            gain = filt[b, spot(0, g), :]
            acc = None
            for k in range(1, 1 + nshort):
                raw = grads[b, spot(k, g), :]
                term = raw * filt[b, spot(k, g), :]
                acc = term if acc is None else acc + term
                grads[b, spot(k, g), :] = raw * gain
            grads[b, spot(0, g), :] = acc

    finish_grads(1)
    to_follow = remote(grads.at[1], gin, p_send.at[0], p_recv.at[0], dev(follow, ctx, dp))
    to_follow.start()

    def send_grads(o):
        z = ctx_at(o)
        return remote(gsent.at[z], rg.at[ctx], g_send.at[o], g_recv.at[ctx], dev(pipe, z, dp))

    def share_grads():
        finish_grads(0)
        remote(grads.at[1], gin, p_send.at[0], p_recv.at[0], dev(prev, ctx, dp)).wait_recv()
        for z in range(nctx):
            for k in range(ntap):
                here = pl.ds(k * nb + z * cb, cb)
                gs[z, k * cb : (k + 1) * cb, :] = grads[0, here, :] + gin[here, :]
            gsent[z] = gs[z].astype(BF16)
        for o in range(1, nctx):
            send_grads(o).start()

    def back_inner(it, _):
        c = chunks - 1 - it
        get_stat(1, chunks, c, mean_of)
        backward(0, c, halo + nrow + halo // 2, 8, back_rows)

        @pl.when(c == 0)
        def _():
            share_grads()

        send_stat(2, c, collect(chunks, c))
        return 0

    lax.fori_loop(0, chunks, back_inner, 0)

    def finish(n, _):
        finish_rows(2 * n)
        finish_rows(2 * n + 1)
        return 0

    def finish_rows(i):
        w = halo + i * 16
        halves = [pl.multiple_of(w + half * SUB, SUB) for half in range(2)]
        scales = [rows[0, pl.ds(h, SUB), :] for h in halves]
        means = [rows[3, pl.ds(h, SUB), :] for h in halves]
        for j in range(nb):
            pieces = []
            for half in range(2):
                here = pl.ds(j // SUB * total * SUB + halves[half] * SUB + j % SUB, SUB, stride=SUB)
                pieces.append(xs[here, :] + scales[half] * (wd_inner[here, :] - saved[0, 0, here, :] * means[half]))
            out[0, pl.ds(pl.multiple_of(i * 16, 16), 16), j * LANES : (j + 1) * LANES] = jnp.concatenate(
                pieces, axis=0
            ).astype(BF16)

    def wind_up(it, _):
        c = chunks - 1 - it
        get_stat(2, chunks, c, mean_of)
        lax.fori_loop(c * (part // 32), (c + 1) * (part // 32), finish, 0)
        return 0

    lax.fori_loop(0, chunks, wind_up, 0)

    for c in range(chunks):
        to_cot(c).wait_send()

    @pl.when(has_up)
    def _():
        to_bot.wait_send()
        to_cbot.wait_send()
        for o in range(ndp):
            to_stat0(2, o, up_z).wait_send()

    @pl.when(has_down)
    def _():
        to_top.wait_send()
        for o in range(ndp):
            to_stat0(0, o, down_z).wait_send()

    for o in range(1, ndp):
        to_stat0(1, o, ctx).wait_send()
    for o in range(1, nctx):
        send_filters(0, o).wait_send()
        send_filters(1, o).wait_send()
    to_prev.wait_send()
    to_follow.wait_send()

    for o in range(1, nctx):
        z = ctx_at(o)
        remote(gsent.at[z], rg.at[z], g_send.at[o], g_recv.at[z], dev(pipe, z, dp)).wait_recv()
    result = gs[ctx]
    for o in range(1, nctx):
        result = result + rg[ctx_at(o)].astype(F32)
    for k in range(ntap):
        for j in range(cb):
            cols = pl.ds(j * LANES, LANES)
            piece = result[k * cb + j : k * cb + j + 1, :]
            if k == 0:
                gain_out[0:1, cols] = piece
            elif k <= nshort:
                short_out[k - 1, 0:1, cols] = piece
            else:
                long_out[k - 1 - nshort, 0:1, cols] = piece

    for o in range(1, nctx):
        send_grads(o).wait_send()


def handed_on(a0, a1, a2, a3, b0, b1, b2, b3, sem):
    half = a0.shape[1] // 2
    pairs = [(a0.at[0, pl.ds(i * half, half), :], b0.at[0, pl.ds(i * half, half), :]) for i in range(2)]
    copies = [
        pltpu.make_async_copy(a, b, sem.at[i]) for i, (a, b) in enumerate(pairs + [(a1, b1), (a2, b2), (a3, b3)])
    ]
    for c in copies:
        c.start()
    for c in copies:
        c.wait()


def swap(values):
    return jnp.transpose(values, (1, 0, 2))


def per_device(mesh, hidden, cotangent, gain_rows, short_taps, long_taps):
    npipe, nctx, ndp = mesh.shape["pipe"], mesh.shape["ctx"], mesh.shape["dp"]
    nrow, chans = hidden.shape[1], hidden.shape[2]
    own = gain_rows.shape[1]
    wide = -(-own // LANES) * LANES
    nshort, nlong = short_taps.shape[1], long_taps.shape[1]
    ntap = 1 + nshort + nlong
    cb = wide // LANES
    nb = nctx * cb
    halo = 2 * (nshort // 3 + nlong - 2)
    total = nrow + 2 * halo
    slab_rows = -(-ntap * cb // 16) * 16
    ahead = next(n for n in (2, 1) if nrow % (16 * n) == 0)
    chunks = next(n for n in (BACK, 1) if nrow % (16 * n) == 0)
    groups = nb // SUB
    nfwd = nshort // 3 - 1 + nlong - 1
    nbwd = nlong - 1 + 3 * (nshort // 3 - 1)

    def widen(values):
        if wide == own:
            return values
        lead = values.shape[:-1]
        blocks = values.reshape(lead + (-1, own))
        blocks = jnp.pad(blocks, [(0, 0)] * (len(lead) + 1) + [(0, wide - own)])
        return blocks.reshape(lead + (-1,))

    def narrow(values):
        if wide == own:
            return values
        lead = values.shape[:-1]
        return values.reshape(lead + (-1, wide))[..., :own].reshape(lead + (-1,))

    cfg = dict(
        npipe=npipe, nctx=nctx, ndp=ndp, nrow=nrow, nb=nb, cb=cb, ntap=ntap, nshort=nshort,
        width=float(chans * ndp), halo=halo, ahead=ahead, chunks=chunks,
    )
    full = nb * LANES
    dma = pltpu.SemaphoreType.DMA
    vmem = pl.BlockSpec(memory_space=pltpu.VMEM)
    anywhere = pl.BlockSpec(memory_space=pl.ANY)
    shapes = (
        jax.ShapeDtypeStruct((1, nrow, full), BF16),
        jax.ShapeDtypeStruct((1, wide), F32),
        jax.ShapeDtypeStruct((nshort, 1, wide), F32),
        jax.ShapeDtypeStruct((nlong, 1, wide), F32),
    )
    outs = pl.pallas_call(
        functools.partial(kernel, cfg),
        out_shape=tuple(pltpu.VMEM(s.shape, s.dtype) for s in shapes),
        in_specs=[anywhere] * 5,
        out_specs=(vmem,) * 4,
        scratch_shapes=[
            pltpu.VMEM((1, wide), F32),
            pltpu.VMEM((nshort, 1, wide), F32),
            pltpu.VMEM((nlong, 1, wide), F32),
            pltpu.VMEM((nrow, full), BF16),
            pltpu.VMEM((halo, full), BF16),
            pltpu.VMEM((halo, full), BF16),
            pltpu.VMEM((nrow, full), BF16),
            pltpu.VMEM((halo, full), BF16),
            pltpu.VMEM((slab_rows, LANES), F32),
            pltpu.VMEM((2, nctx, slab_rows, LANES), F32),
            pltpu.VMEM((2, ntap * nb, LANES), F32),
            pltpu.VMEM((2, nshort * nb, LANES), F32),
            pltpu.VMEM((2, ntap * nb, LANES), F32),
            pltpu.VMEM((ntap * nb, LANES), F32),
            pltpu.VMEM((nctx, slab_rows, LANES), F32),
            pltpu.VMEM((nctx, slab_rows, LANES), BF16),
            pltpu.VMEM((nctx, slab_rows, LANES), BF16),
            pltpu.VMEM((total * nb, LANES), F32),
            pltpu.VMEM((total * nb, LANES), F32),
            pltpu.VMEM((total * nb, LANES), F32),
            pltpu.VMEM((total * nb, LANES), F32),
            pltpu.VMEM((total * nb, LANES), F32),
            pltpu.VMEM((2, 6, total * nb, LANES), F32),
            pltpu.VMEM((total * SUB, LANES), F32),
            pltpu.VMEM((2 * groups * nfwd * SUB, LANES), F32),
            pltpu.VMEM((2 * groups * nbwd * SUB, LANES), F32),
            pltpu.VMEM((SUB, LANES), F32),
            pltpu.VMEM((3, ndp, SUB, LANES), F32),
            pltpu.VMEM((3, ahead, SUB, LANES), F32),
            pltpu.VMEM((3, ahead, ndp, SUB, LANES), F32),
            pltpu.VMEM((4, total, LANES), F32),
            dma((chunks,)),
            dma((3,)),
            dma((3,)),
            dma((3,)),
            dma((chunks,)),
            dma((chunks,)),
            dma((2, nctx)),
            dma((2, nctx)),
            dma((1,)),
            dma((1,)),
            dma((nctx,)),
            dma((nctx,)),
            dma((3, ndp)),
            dma((3, ndp)),
            dma((3, ahead, ndp)),
            dma((3, ahead, ndp)),
        ],
        compiler_params=pltpu.CompilerParams(
            collective_id=0, has_side_effects=True, vmem_limit_bytes=62 * 1024 * 1024 - 1400 * 1024
        ),
        name="relay",
    )(widen(hidden), widen(cotangent), widen(gain_rows), swap(widen(short_taps)), swap(widen(long_taps)))
    outs = pl.pallas_call(
        handed_on,
        out_shape=shapes,
        in_specs=[vmem] * 4,
        out_specs=(anywhere,) * 4,
        scratch_shapes=[dma((5,))],
        compiler_params=pltpu.CompilerParams(vmem_limit_bytes=4 * 1024 * 1024),
        name="handed_on",
    )(*outs)
    return tuple(narrow(o) for o in (outs[0], outs[1], swap(outs[2]), swap(outs[3])))


def solution(mesh):
    in_specs = (
        P("pipe", "ctx", "dp"),
        P("pipe", "ctx", "dp"),
        P("pipe", ("dp", "ctx")),
        P("pipe", None, ("dp", "ctx")),
        P("pipe", None, ("dp", "ctx")),
    )
    out_specs = (
        P("pipe", "ctx", "dp"),
        P("pipe", ("dp", "ctx")),
        P("pipe", None, ("dp", "ctx")),
        P("pipe", None, ("dp", "ctx")),
    )
    return jax.shard_map(
        functools.partial(per_device, mesh), mesh=mesh, in_specs=in_specs, out_specs=out_specs, check_vma=False
    )
```

```python
import functools

import jax
import jax.numpy as jnp
from jax import lax
from jax.experimental import pallas as pl
from jax.experimental.pallas import tpu as pltpu
from jax.sharding import PartitionSpec as P

MESH = pl.DeviceIdType.MESH
F32 = jnp.float32
BF16 = jnp.bfloat16
LANES = 128
SUB = 8
EPS = 1e-05
BACK = 2


def kernel(
    cfg,
    hid,
    cot,
    gain_hbm,
    short_hbm,
    long_hbm,
    out,
    gain_out,
    short_out,
    long_out,
    gain_in,
    short_in,
    long_in,
    hbuf,
    htop,
    hbot,
    cbuf,
    cbot,
    slab,
    fr,
    filt,
    fold,
    grads,
    gin,
    gs,
    gsent,
    rg,
    xs,
    ys,
    zs,
    wd_outer,
    wd_inner,
    saved,
    parts,
    fstate,
    bstate,
    st0_send,
    st0_recv,
    st_send,
    st_recv,
    rows,
    in_sem,
    small_sem,
    halo_send,
    halo_recv,
    c_send,
    c_recv,
    f_send,
    f_recv,
    p_send,
    p_recv,
    g_send,
    g_recv,
    s0_send,
    s0_recv,
    s_send,
    s_recv,
):
    npipe, nctx, ndp = cfg["npipe"], cfg["nctx"], cfg["ndp"]
    nrow, nb, cb, ntap, nshort, width = (
        cfg["nrow"], cfg["nb"], cfg["cb"], cfg["ntap"], cfg["nshort"], cfg["width"],
    )
    ahead, chunks = cfg["ahead"], cfg["chunks"]
    taps = nshort // 3
    nlong = ntap - 1 - nshort
    halo = cfg["halo"]
    total = nrow + 2 * halo
    part = nrow // chunks
    reach = nrow // ahead + (halo if ahead == 2 else 2 * halo)
    ahead_rows = next(n for n in (24, 16, 8) if reach % n == 0)
    back_rows = next(n for n in (32, 16) if part % n == 0)
    groups = nb // SUB
    edge = halo // SUB
    slabs = SUB // cb if cb < SUB and SUB % cb == 0 else nctx
    slabs = min(slabs, nctx)
    teams = nctx // slabs
    nfwd = taps - 1 + nlong - 1
    nbwd = nlong - 1 + 3 * (taps - 1)
    pipe, ctx, dp = lax.axis_index("pipe"), lax.axis_index("ctx"), lax.axis_index("dp")
    prev = lax.rem(pipe + npipe - 1, npipe)
    follow = lax.rem(pipe + 1, npipe)

    def ctx_at(o):
        return lax.rem(ctx + o, nctx)

    def dp_at(o):
        return lax.rem(dp + o, ndp)

    def team_at(o):
        team = lax.rem(ctx // slabs + o // slabs, teams)
        return team * slabs + lax.rem(lax.rem(ctx, slabs) + o % slabs, slabs)

    def dev(p, z, d):
        return {"pipe": p, "ctx": z, "dp": d}

    def remote(src, dst, ss, rs, where):
        return pltpu.make_async_remote_copy(
            src_ref=src, dst_ref=dst, send_sem=ss, recv_sem=rs, device_id=where, device_id_type=MESH
        )

    barrier = pltpu.get_barrier_semaphore()
    peers = [(pipe, ctx_at(o), dp) for o in range(1, nctx)]
    for d in range(1, ndp):
        for o in sorted({0, 1 % nctx, (nctx - 1) % nctx}):
            peers.append((pipe, ctx_at(o), dp_at(d)))
    peers += [(prev, ctx, dp), (follow, ctx, dp), (follow, ctx_at(1), dp)]
    for p, z, d in peers:
        pl.semaphore_signal(barrier, inc=1, device_id=dev(p, z, d), device_id_type=MESH)

    def rows_of(c):
        return pl.ds(c * part, part)

    def load_hid(c):
        return pltpu.make_async_copy(hid.at[0, rows_of(c), :], hbuf.at[rows_of(c), :], in_sem.at[c])

    small = [
        pltpu.make_async_copy(a, b, small_sem.at[i])
        for i, (a, b) in enumerate(((gain_hbm, gain_in), (short_hbm, short_in), (long_hbm, long_in)))
    ]
    for copy in small:
        copy.start()
    for c in range(chunks):
        load_hid(c).start()

    zero = jnp.zeros((SUB, LANES), F32)
    for i in range(2 * groups * nfwd):
        fstate[i * SUB : (i + 1) * SUB, :] = zero
    for i in range(2 * groups * nbwd):
        bstate[i * SUB : (i + 1) * SUB, :] = zero
    for i in range(2 * ntap * groups):
        grads[i // (ntap * groups), i % (ntap * groups) * SUB : (i % (ntap * groups) + 1) * SUB, :] = zero

    lane = lax.broadcasted_iota(jnp.int32, (SUB, LANES), 1)

    def spread(dst, first, block):
        for half in range(2):
            piece = block[half * SUB : (half + 1) * SUB, :]
            start = (first + half * SUB) * SUB
            for j in range(nb):
                dst[pl.ds(j // SUB * total * SUB + start + j % SUB, SUB, stride=SUB), :] = piece[:, j * LANES : (j + 1) * LANES]

    def squares(stat, first, block):
        for half in range(2):
            acc = None
            for j in range(nb):
                piece = block[half * SUB : (half + 1) * SUB, j * LANES : (j + 1) * LANES]
                acc = piece * piece if acc is None else acc + piece * piece
            value = jnp.sum(acc, axis=1, keepdims=True)
            stat = jnp.where(lane == first // SUB + half, value, stat)
        return stat

    def take_hidden(i, stat):
        block = hbuf[pl.ds(pl.multiple_of(i * 16, 16), 16), :].astype(F32)
        spread(xs, halo + i * 16, block)
        return squares(stat, halo + i * 16, block)

    for copy in small:
        copy.wait()
    for k in range(ntap):
        src, row = (gain_in, 0) if k == 0 else ((short_in, k - 1) if k <= nshort else (long_in, k - 1 - nshort))
        for j in range(cb):
            cols = pl.ds(j * LANES, LANES)
            piece = src[row : row + 1, cols] if k == 0 else src[row, 0:1, cols]
            slab[k * cb + j : k * cb + j + 1, :] = piece
    pad = slab.shape[0] - ntap * cb
    if pad:
        slab[ntap * cb :, :] = jnp.zeros((pad, LANES), F32)
        for z in range(nctx):
            gs[z, ntap * cb :, :] = jnp.zeros((pad, LANES), F32)
    fr[0, ctx] = slab[...]
    stat = zero
    for c in range(chunks):
        load_hid(c).wait()
        stat = lax.fori_loop(c * part // 16, (c + 1) * part // 16, take_hidden, stat)
    st0_send[...] = stat
    st0_recv[1, dp] = stat

    pl.semaphore_wait(barrier, len(peers))

    up_z = lax.max(ctx - 1, 0)
    down_z = lax.min(ctx + 1, nctx - 1)
    head, tail = pl.ds(0, halo), pl.ds(nrow - halo, halo)
    to_bot = remote(hbuf.at[head, :], hbot, halo_send.at[0], halo_recv.at[0], dev(pipe, up_z, dp))
    to_top = remote(hbuf.at[tail, :], htop, halo_send.at[1], halo_recv.at[1], dev(pipe, down_z, dp))
    to_cbot = remote(cot.at[0, head, :], cbot, halo_send.at[2], halo_recv.at[2], dev(prev, up_z, dp))
    has_up, has_down = ctx > 0, ctx < nctx - 1

    def send_filters(b, o):
        mine = fr.at[1, ctx] if b else slab
        return remote(mine, fr.at[b, ctx], f_send.at[b, o], f_recv.at[b, ctx], dev(pipe, team_at(o), dp))

    def wait_filters(b, o):
        there = team_at(o)
        remote(slab, fr.at[b, there], f_send.at[b, o], f_recv.at[b, there], dev(pipe, there, dp)).wait_recv()

    to_prev = remote(slab, fr.at[1, ctx], f_send.at[1, 0], f_recv.at[1, ctx], dev(prev, ctx, dp))

    def to_stat0(slot, o, z):
        return remote(st0_send, st0_recv.at[slot, dp], s0_send.at[slot, o], s0_recv.at[slot, dp], dev(pipe, z, dp_at(o)))

    def from_stat0(slot, o, z):
        there = dp_at(o)
        return remote(
            st0_send, st0_recv.at[slot, there], s0_send.at[slot, o], s0_recv.at[slot, there], dev(pipe, z, there)
        )

    for o in range(1, ndp):
        to_stat0(1, o, ctx).start()

    @pl.when(has_down)
    def _():
        for o in range(ndp):
            to_stat0(0, o, down_z).start()

    @pl.when(has_up)
    def _():
        for o in range(ndp):
            to_stat0(2, o, up_z).start()

    for o in range(nctx - 1, 1, -1):
        send_filters(0, o).start()

    @pl.when(has_down)
    def _():
        to_top.start()

    send_filters(0, 1).start()

    @pl.when(has_up)
    def _():
        to_bot.start()
        to_cbot.start()

    def to_cot(c):
        return remote(
            cot.at[0, rows_of(c), :], cbuf.at[rows_of(c), :], c_send.at[c], c_recv.at[c], dev(prev, ctx, dp)
        )

    to_prev.start()
    for c in range(chunks - 1, -1, -1):
        to_cot(c).start()

    @pl.when(has_up)
    def _():
        remote(htop, htop, halo_send.at[1], halo_recv.at[1], dev(pipe, up_z, dp)).wait_recv()
        for o in range(ndp):
            from_stat0(0, o, up_z).wait_recv()

    @pl.when(jnp.logical_not(has_up))
    def _():
        htop[...] = jnp.zeros(htop.shape, BF16)
        for d in range(ndp):
            st0_recv[0, d] = zero

    @pl.when(has_down)
    def _():
        remote(hbot, hbot, halo_send.at[0], halo_recv.at[0], dev(pipe, down_z, dp)).wait_recv()
        for o in range(ndp):
            from_stat0(2, o, down_z).wait_recv()

    @pl.when(jnp.logical_not(has_down))
    def _():
        hbot[...] = jnp.zeros(hbot.shape, BF16)
        for d in range(ndp):
            st0_recv[2, d] = zero

    remote(slab, fr.at[1, ctx], f_send.at[1, 0], f_recv.at[1, ctx], dev(follow, ctx, dp)).wait_recv()
    for o in range(1, nctx):
        send_filters(1, o).start()

    spread(xs, 0, htop[...].astype(F32))
    spread(xs, halo + nrow, hbot[...].astype(F32))

    def row_scale(value):
        return lax.rsqrt(value / width + EPS)

    def mean_of(value):
        return value / width

    def put_rows(stage, at_octet, value, i):
        column = jnp.sum(jnp.where(lane == i, value, 0.0), axis=1, keepdims=True)
        rows[stage, pl.ds(pl.multiple_of(at_octet * SUB, SUB), SUB), :] = jnp.broadcast_to(column, (SUB, LANES))

    for o in range(1, ndp):
        from_stat0(1, o, ctx).wait_recv()
    sums = []
    for slot in range(3):
        value = st0_recv[slot, 0]
        for d in range(1, ndp):
            value = value + st0_recv[slot, d]
        sums.append(row_scale(value))
    for i in range(edge):
        put_rows(0, i, sums[0], i + nrow // SUB)
        put_rows(0, edge + nrow // SUB + i, sums[2], i + edge)
    for i in range(edge, edge + nrow // SUB):
        put_rows(0, i, sums[1], i)

    def first_octet(many, c):
        return jnp.where(c == 0, 0, edge + nrow // SUB // many * c)

    def span(many):
        return nrow // SUB // many + edge

    def send_stat(stage, c, value):
        st_send[stage, c] = value
        st_recv[stage, c, dp] = value
        for o in range(1, ndp):
            remote(
                st_send.at[stage, c], st_recv.at[stage, c, dp], s_send.at[stage, c, o], s_recv.at[stage, c, dp],
                dev(pipe, ctx, dp_at(o)),
            ).start()

    def get_stat(stage, many, c, fn):
        for o in range(1, ndp):
            there = dp_at(o)
            remote(
                st_send.at[stage, c], st_recv.at[stage, c, there], s_send.at[stage, c, o], s_recv.at[stage, c, there],
                dev(pipe, ctx, there),
            ).wait()
        value = st_recv[stage, c, 0]
        for d in range(1, ndp):
            value = value + st_recv[stage, c, d]
        value = fn(value)
        base = first_octet(many, c)
        for k in range(span(many)):
            put_rows(stage + 1, base + k, value, base + k)

    def collect(many, c):
        base = first_octet(many, c)
        value = zero
        for n in range(span(many)):
            acc = None
            for k in range(SUB):
                piece = parts[pl.ds((base + n) * SUB * SUB + k, SUB, stride=SUB), :]
                acc = piece if acc is None else acc + piece
            value = jnp.where(lane == base + n, jnp.sum(acc, axis=1, keepdims=True), value)
        return value

    per = groups // teams

    def spot(k, g):
        return pl.ds(k * nb + g * SUB if isinstance(g, int) else pl.multiple_of(k * nb + g * SUB, SUB), SUB)

    def build_filters(b, team):
        for n in range(per):
            g = team * per + n
            first = n * SUB // cb
            many = max(SUB // cb, 1)
            for k in range(ntap):
                if cb >= SUB:
                    z, row = n * SUB // cb, n * SUB % cb
                    value = fr[b, team * slabs + z, k * cb + row : k * cb + row + SUB, :]
                else:
                    value = jnp.concatenate(
                        [fr[b, team * slabs + first + s, k * cb : (k + 1) * cb, :] for s in range(many)], axis=0
                    )
                filt[b, spot(k, g), :] = value
                if k == 0:
                    gain = value
                elif k <= nshort:
                    fold[b, spot(k - 1, g), :] = value * gain

    def at(w, g):
        return pl.ds(pl.multiple_of((g * total + w) * SUB, SUB), SUB)

    def row_of(stage, w):
        return jnp.broadcast_to(rows[stage, pl.ds(w, 1), :], (SUB, LANES))

    def kept(ref, b, g, count, i):
        return ref.at[pl.ds(((b * groups + g) * count + i) * SUB, SUB), :]

    def add_part(w, g, value):
        here = at(w, 0)
        parts[here, :] = value if g == 0 else parts[here, :] + value

    def forward(b, c, start, unroll):
        part, chunks = nrow // ahead, ahead
        lo = jnp.where(c == 0, start, halo + part * c)
        hi = jnp.where(c == chunks - 1, total, halo + part * (c + 1))

        def step(it, _):
            for g in range(groups):
                short = [fold[b, spot(k, g), :] for k in range(nshort)]
                long = [filt[b, spot(1 + nshort + k, g), :] for k in range(nlong)]
                held = [kept(fstate, b, g, nfwd, i) for i in range(nfwd)]
                lag = [ref[...] for ref in held[: taps - 1]]
                past = [ref[...] for ref in held[taps - 1 :]]
                for u in range(unroll):
                    w = lo + it * unroll + u
                    x = (xs if b == 0 else ys)[at(w, g), :]
                    xh = x * row_of(b, w)
                    seq = [xh] + lag
                    streams = []
                    for j in range(3):
                        value = short[taps * j] * seq[0]
                        for i in range(1, taps):
                            value = value + short[taps * j + i] * seq[i]
                        streams.append(value)
                    products = [streams[1] * streams[2]] + past
                    mix = long[0] * products[0]
                    for i in range(1, nlong):
                        mix = mix + long[i] * products[i]
                    for n, value in enumerate((xh, streams[0], streams[1], streams[2], mix, products[0])):
                        saved[b, n, at(w, g), :] = value
                    if b == 0:
                        inner = (x + streams[0] * mix).astype(BF16).astype(F32)
                        ys[at(w, g), :] = inner
                        add_part(w, g, inner * inner)
                    lag, past = seq[:-1], products[:-1]
                for ref, value in zip(held, lag + past):
                    ref[...] = value
            return 0

        lax.fori_loop(0, (hi - lo) // unroll, step, 0)

    for o in range(1, nctx):
        wait_filters(0, o)
    for n in range(teams):
        build_filters(0, n)

    def ahead_inner(c, _):
        forward(0, c, 0, ahead_rows)
        send_stat(0, c, collect(ahead, c))
        return 0

    lax.fori_loop(0, ahead, ahead_inner, 0)

    for o in range(1, nctx):
        wait_filters(1, o)
    for n in range(teams):
        build_filters(1, n)

    def ahead_outer(c, _):
        get_stat(0, ahead, c, row_scale)
        forward(1, c, 0, ahead_rows)
        return 0

    lax.fori_loop(0, ahead, ahead_outer, 0)

    @pl.when(has_down)
    def _():
        remote(cbot, cbot, halo_send.at[2], halo_recv.at[2], dev(follow, down_z, dp)).wait_recv()

    @pl.when(jnp.logical_not(has_down))
    def _():
        cbot[...] = jnp.zeros(cbot.shape, BF16)

    spread(zs, halo + nrow, cbot[...].astype(F32))

    def take_cot(i, _):
        spread(zs, halo + i * 16, cbuf[pl.ds(pl.multiple_of(i * 16, 16), 16), :].astype(F32))
        return 0

    def backward(b, c, top, brief, unroll):
        lo = halo + part * c
        hi = lo + part

        def one(g, w, short, long, state, acc):
            dmix_next, ds_next = state
            here = at(w, g)
            up = zs[here, :]
            if b == 0:
                up = up + row_of(1, w) * (wd_outer[here, :] - saved[1, 0, here, :] * row_of(2, w))
                xs[here, :] = up
            xh, query, key, value, mix, product = [saved[b, n, here, :] for n in range(6)]
            dmix = [up * query] + dmix_next
            dprod = long[0] * dmix[0]
            for i in range(1, nlong):
                dprod = dprod + long[i] * dmix[i]
            ds = [[up * mix] + ds_next[0], [dprod * value] + ds_next[1], [dprod * key] + ds_next[2]]
            weighted = None
            for j in range(3):
                for i in range(taps):
                    term = short[taps * j + i] * ds[j][i]
                    weighted = term if weighted is None else weighted + term
            (wd_outer if b == 1 else wd_inner)[here, :] = weighted
            add_part(w, g, xh * weighted)
            if acc is not None:
                fresh = []
                for j in range(3):
                    for i in range(taps):
                        fresh.append(acc[taps * j + i] + xh * ds[j][i])
                for i in range(nlong):
                    fresh.append(acc[nshort + i] + product * dmix[i])
                acc = fresh
            return (dmix[:-1], [d[:-1] for d in ds]), acc

        def flat(state):
            return list(state[0]) + [v for d in state[1] for v in d]

        def unflat(vals):
            n = nlong - 1
            rest = vals[n:]
            m = taps - 1
            return list(vals[:n]), [list(rest[j * m : (j + 1) * m]) for j in range(3)]

        def rows_back(high, many, summed):
            def step(it, _):
                for g in range(groups):
                    short = [fold[b, spot(k, g), :] for k in range(nshort)]
                    long = [filt[b, spot(1 + nshort + k, g), :] for k in range(nlong)]
                    held = [kept(bstate, b, g, nbwd, i) for i in range(nbwd)]
                    state = unflat([ref[...] for ref in held])
                    acc = [grads[b, spot(k, g), :] for k in range(1, ntap)] if summed else None
                    for u in range(many):
                        state, acc = one(g, high - 1 - it * many - u, short, long, state, acc)
                    for ref, value in zip(held, flat(state)):
                        ref[...] = value
                    if summed:
                        for k in range(1, ntap):
                            grads[b, spot(k, g), :] = acc[k - 1]
                return 0

            return step

        extra = jnp.where(c == chunks - 1, (top - halo - nrow) // brief, 0)
        lax.fori_loop(0, extra, rows_back(top, brief, False), 0)
        lax.fori_loop(0, part // unroll, rows_back(hi, unroll, True), 0)

    def back_outer(it, _):
        c = chunks - 1 - it
        remote(
            cbuf.at[rows_of(c), :], cbuf.at[rows_of(c), :], c_send.at[c], c_recv.at[c], dev(follow, ctx, dp)
        ).wait_recv()
        lax.fori_loop(c * (part // 16), (c + 1) * (part // 16), take_cot, 0)
        backward(1, c, total, 8, back_rows)
        send_stat(1, c, collect(chunks, c))
        return 0

    lax.fori_loop(0, chunks, back_outer, 0)

    def finish_grads(b):
        for g in range(groups):
            gain = filt[b, spot(0, g), :]
            acc = None
            for k in range(1, 1 + nshort):
                raw = grads[b, spot(k, g), :]
                term = raw * filt[b, spot(k, g), :]
                acc = term if acc is None else acc + term
                grads[b, spot(k, g), :] = raw * gain
            grads[b, spot(0, g), :] = acc

    finish_grads(1)
    to_follow = remote(grads.at[1], gin, p_send.at[0], p_recv.at[0], dev(follow, ctx, dp))
    to_follow.start()

    def send_grads(o):
        z = ctx_at(o)
        return remote(gsent.at[z], rg.at[ctx], g_send.at[o], g_recv.at[ctx], dev(pipe, z, dp))

    def share_grads():
        finish_grads(0)
        remote(grads.at[1], gin, p_send.at[0], p_recv.at[0], dev(prev, ctx, dp)).wait_recv()
        for z in range(nctx):
            for k in range(ntap):
                here = pl.ds(k * nb + z * cb, cb)
                gs[z, k * cb : (k + 1) * cb, :] = grads[0, here, :] + gin[here, :]
            gsent[z] = gs[z].astype(BF16)
        for o in range(1, nctx):
            send_grads(o).start()

    def back_inner(it, _):
        c = chunks - 1 - it
        get_stat(1, chunks, c, mean_of)
        backward(0, c, halo + nrow + halo // 2, 8, back_rows)

        @pl.when(c == 0)
        def _():
            share_grads()

        send_stat(2, c, collect(chunks, c))
        return 0

    lax.fori_loop(0, chunks, back_inner, 0)

    def finish(i, _):
        w = halo + i * 16
        halves = [pl.multiple_of(w + half * SUB, SUB) for half in range(2)]
        scales = [rows[0, pl.ds(h, SUB), :] for h in halves]
        means = [rows[3, pl.ds(h, SUB), :] for h in halves]
        for j in range(nb):
            pieces = []
            for half in range(2):
                here = pl.ds(j // SUB * total * SUB + halves[half] * SUB + j % SUB, SUB, stride=SUB)
                pieces.append(xs[here, :] + scales[half] * (wd_inner[here, :] - saved[0, 0, here, :] * means[half]))
            out[0, pl.ds(pl.multiple_of(i * 16, 16), 16), j * LANES : (j + 1) * LANES] = jnp.concatenate(
                pieces, axis=0
            ).astype(BF16)
        return 0

    def wind_up(it, _):
        c = chunks - 1 - it
        get_stat(2, chunks, c, mean_of)
        lax.fori_loop(c * (part // 16), (c + 1) * (part // 16), finish, 0)
        return 0

    lax.fori_loop(0, chunks, wind_up, 0)

    for c in range(chunks):
        to_cot(c).wait_send()

    @pl.when(has_up)
    def _():
        to_bot.wait_send()
        to_cbot.wait_send()
        for o in range(ndp):
            to_stat0(2, o, up_z).wait_send()

    @pl.when(has_down)
    def _():
        to_top.wait_send()
        for o in range(ndp):
            to_stat0(0, o, down_z).wait_send()

    for o in range(1, ndp):
        to_stat0(1, o, ctx).wait_send()
    for o in range(1, nctx):
        send_filters(0, o).wait_send()
        send_filters(1, o).wait_send()
    to_prev.wait_send()
    to_follow.wait_send()

    for o in range(1, nctx):
        z = ctx_at(o)
        remote(gsent.at[z], rg.at[z], g_send.at[o], g_recv.at[z], dev(pipe, z, dp)).wait_recv()
    result = gs[ctx]
    for o in range(1, nctx):
        result = result + rg[ctx_at(o)].astype(F32)
    for k in range(ntap):
        for j in range(cb):
            cols = pl.ds(j * LANES, LANES)
            piece = result[k * cb + j : k * cb + j + 1, :]
            if k == 0:
                gain_out[0:1, cols] = piece
            elif k <= nshort:
                short_out[k - 1, 0:1, cols] = piece
            else:
                long_out[k - 1 - nshort, 0:1, cols] = piece

    for o in range(1, nctx):
        send_grads(o).wait_send()


def handed_on(a0, a1, a2, a3, b0, b1, b2, b3, sem):
    pairs = [(a0, b0), (a1, b1), (a2, b2), (a3, b3)]
    copies = [pltpu.make_async_copy(a, b, sem.at[i]) for i, (a, b) in enumerate(pairs)]
    for c in copies:
        c.start()
    for c in copies:
        c.wait()


def swap(values):
    return jnp.transpose(values, (1, 0, 2))


def per_device(mesh, hidden, cotangent, gain_rows, short_taps, long_taps):
    npipe, nctx, ndp = mesh.shape["pipe"], mesh.shape["ctx"], mesh.shape["dp"]
    nrow, chans = hidden.shape[1], hidden.shape[2]
    own = gain_rows.shape[1]
    wide = -(-own // LANES) * LANES
    nshort, nlong = short_taps.shape[1], long_taps.shape[1]
    ntap = 1 + nshort + nlong
    cb = wide // LANES
    nb = nctx * cb
    halo = 2 * (nshort // 3 + nlong - 2)
    total = nrow + 2 * halo
    slab_rows = -(-ntap * cb // 16) * 16
    ahead = next(n for n in (2, 1) if nrow % (16 * n) == 0)
    chunks = next(n for n in (BACK, 1) if nrow % (16 * n) == 0)
    groups = nb // SUB
    nfwd = nshort // 3 - 1 + nlong - 1
    nbwd = nlong - 1 + 3 * (nshort // 3 - 1)

    def widen(values):
        if wide == own:
            return values
        lead = values.shape[:-1]
        blocks = values.reshape(lead + (-1, own))
        blocks = jnp.pad(blocks, [(0, 0)] * (len(lead) + 1) + [(0, wide - own)])
        return blocks.reshape(lead + (-1,))

    def narrow(values):
        if wide == own:
            return values
        lead = values.shape[:-1]
        return values.reshape(lead + (-1, wide))[..., :own].reshape(lead + (-1,))

    cfg = dict(
        npipe=npipe, nctx=nctx, ndp=ndp, nrow=nrow, nb=nb, cb=cb, ntap=ntap, nshort=nshort,
        width=float(chans * ndp), halo=halo, ahead=ahead, chunks=chunks,
    )
    full = nb * LANES
    dma = pltpu.SemaphoreType.DMA
    vmem = pl.BlockSpec(memory_space=pltpu.VMEM)
    anywhere = pl.BlockSpec(memory_space=pl.ANY)
    shapes = (
        jax.ShapeDtypeStruct((1, nrow, full), BF16),
        jax.ShapeDtypeStruct((1, wide), F32),
        jax.ShapeDtypeStruct((nshort, 1, wide), F32),
        jax.ShapeDtypeStruct((nlong, 1, wide), F32),
    )
    outs = pl.pallas_call(
        functools.partial(kernel, cfg),
        out_shape=tuple(pltpu.VMEM(s.shape, s.dtype) for s in shapes),
        in_specs=[anywhere] * 5,
        out_specs=(vmem,) * 4,
        scratch_shapes=[
            pltpu.VMEM((1, wide), F32),
            pltpu.VMEM((nshort, 1, wide), F32),
            pltpu.VMEM((nlong, 1, wide), F32),
            pltpu.VMEM((nrow, full), BF16),
            pltpu.VMEM((halo, full), BF16),
            pltpu.VMEM((halo, full), BF16),
            pltpu.VMEM((nrow, full), BF16),
            pltpu.VMEM((halo, full), BF16),
            pltpu.VMEM((slab_rows, LANES), F32),
            pltpu.VMEM((2, nctx, slab_rows, LANES), F32),
            pltpu.VMEM((2, ntap * nb, LANES), F32),
            pltpu.VMEM((2, nshort * nb, LANES), F32),
            pltpu.VMEM((2, ntap * nb, LANES), F32),
            pltpu.VMEM((ntap * nb, LANES), F32),
            pltpu.VMEM((nctx, slab_rows, LANES), F32),
            pltpu.VMEM((nctx, slab_rows, LANES), BF16),
            pltpu.VMEM((nctx, slab_rows, LANES), BF16),
            pltpu.VMEM((total * nb, LANES), F32),
            pltpu.VMEM((total * nb, LANES), F32),
            pltpu.VMEM((total * nb, LANES), F32),
            pltpu.VMEM((total * nb, LANES), F32),
            pltpu.VMEM((total * nb, LANES), F32),
            pltpu.VMEM((2, 6, total * nb, LANES), F32),
            pltpu.VMEM((total * SUB, LANES), F32),
            pltpu.VMEM((2 * groups * nfwd * SUB, LANES), F32),
            pltpu.VMEM((2 * groups * nbwd * SUB, LANES), F32),
            pltpu.VMEM((SUB, LANES), F32),
            pltpu.VMEM((3, ndp, SUB, LANES), F32),
            pltpu.VMEM((3, ahead, SUB, LANES), F32),
            pltpu.VMEM((3, ahead, ndp, SUB, LANES), F32),
            pltpu.VMEM((4, total, LANES), F32),
            dma((chunks,)),
            dma((3,)),
            dma((3,)),
            dma((3,)),
            dma((chunks,)),
            dma((chunks,)),
            dma((2, nctx)),
            dma((2, nctx)),
            dma((1,)),
            dma((1,)),
            dma((nctx,)),
            dma((nctx,)),
            dma((3, ndp)),
            dma((3, ndp)),
            dma((3, ahead, ndp)),
            dma((3, ahead, ndp)),
        ],
        compiler_params=pltpu.CompilerParams(
            collective_id=0, has_side_effects=True, vmem_limit_bytes=62 * 1024 * 1024 - 1400 * 1024
        ),
        name="relay",
    )(widen(hidden), widen(cotangent), widen(gain_rows), swap(widen(short_taps)), swap(widen(long_taps)))
    outs = pl.pallas_call(
        handed_on,
        out_shape=shapes,
        in_specs=[vmem] * 4,
        out_specs=(anywhere,) * 4,
        scratch_shapes=[dma((4,))],
        compiler_params=pltpu.CompilerParams(vmem_limit_bytes=4 * 1024 * 1024),
        name="handed_on",
    )(*outs)
    return tuple(narrow(o) for o in (outs[0], outs[1], swap(outs[2]), swap(outs[3])))


def solution(mesh):
    in_specs = (
        P("pipe", "ctx", "dp"),
        P("pipe", "ctx", "dp"),
        P("pipe", ("dp", "ctx")),
        P("pipe", None, ("dp", "ctx")),
        P("pipe", None, ("dp", "ctx")),
    )
    out_specs = (
        P("pipe", "ctx", "dp"),
        P("pipe", ("dp", "ctx")),
        P("pipe", None, ("dp", "ctx")),
        P("pipe", None, ("dp", "ctx")),
    )
    return jax.shard_map(
        functools.partial(per_device, mesh), mesh=mesh, in_specs=in_specs, out_specs=out_specs, check_vma=False
    )
```
